32 devices in a mesh: ground: 16 (over z, x, core), pair: 2 (over y).
Axes of the slice: x: 2, y: 2, z: 4, core: 2. Of those that a mesh axis runs over, the one named last changes fastest.
Arguments:
- coregistered_sweeps: bfloat16 [2, 16, 512, 2, 512], P('pair', 'ground'), may hold values from -6 to 6
- shard_opening_height: int32 [1024], P('ground'), may hold values from 0 to 496
- shard_goal_patch: int32 [1024, 1], P('ground'), may hold values from 0 to 15; in each aligned block of 64 rows (0 to 63, 64 to 127, ...) at most 8 rows name the same one
- shard_patch_place: int32 [1024], P('ground'), may hold values from 0 to 31
Outputs:
- filtered: float32 [2, 1, 16, 2, 64, 64], P('pair', None, 'ground')
The draws below stay inside these ranges and needn't reach their ends.
Inputs may be any that keep to these rules, and one draw needn't show every extreme that they name: `shard_goal_patch`: among the 64 pieces of the bursts of one ground index, at most 8 name the same ground tile.
All inputs are finite; a program needn't handle non-finite values.
Results may differ from the reference program's by a relative error of at most 0.0023.
Values may be sent and summed in bfloat16 or wider, within the bound.
A program may use at most 320 MiB of HBM per device.

```python
import math
import jax
import jax.numpy as jnp
import numpy as np
from jax import lax

LOOK_ROWS = 4
LOOK_COLS = 16
SWEEP_HEIGHT = 512
SHARD_HEIGHT = 16
PIECE_DEV = 64
TILE_ROWS = 256
TILE_COLS = 1024
SWEEP_WIDTH = 512
PATCH_SHARD_LEVEL = 16
SLOTS = 32
SHARD_OVERALL = 1024
CAP = 8
PAIR_DEV = 1
N_GROUND = 16
N_PAIR = 2


def plant(entries, key, low, high):
    place = [jax.random.randint(jax.random.fold_in(key, axis), (), 0, length) for axis, length in enumerate(entries.shape)]
    widest = entries.shape.index(max(entries.shape))
    next_to = place[:widest] + [(place[widest] + 1) % entries.shape[widest]] + place[widest + 1:]
    return entries.at[tuple(place)].set(low).at[tuple(next_to)].set(high)


def levels(key, shape, cuts, least, high):
    def one(axis_at, parts):
        steps = jax.random.uniform(jax.random.fold_in(jax.random.fold_in(key, 6), axis_at), (parts,), jnp.float32, least / len(cuts), high / len(cuts))
        return jnp.repeat(jnp.exp(steps), shape[axis_at] // parts).reshape((-1,) + (1,) * (len(shape) - axis_at - 1))

    gain = one(*cuts[0])
    for cut in cuts[1:]:
        gain = gain * one(*cut)
    return gain


def assign_block(stream_key, own, number, rows, amount, top, bound, lean):
    order = jax.random.permutation(stream_key, amount)
    heavy_load, common = load_shares(amount, rows * top, bound, lean, True), load_shares(amount, rows * top, bound, lean, False)
    places = jnp.arange(amount)

    def named(sizes, rotation):
        used = int((sizes > 0).sum())
        fixed = max(1, used // 4)
        moved = fixed + (places - fixed + rotation * (used - fixed)) % max(1, amount - fixed)
        return jnp.zeros((amount,), jnp.int32).at[order[jnp.where(places < fixed, places, moved)]].set(jnp.asarray(sizes, jnp.int32))

    sizes = jnp.where(number % 4 == 0, named(heavy_load, number // 4), named(common, number - number // 4 - 1))
    mixed = jax.random.permutation(jax.random.fold_in(own, 3), amount)
    source_of, receiver = mixed[0:amount // 2 * 2:2], mixed[1:amount // 2 * 2:2]
    margin = jnp.minimum(sizes[source_of] - 1, bound - sizes[receiver]) // 2
    margin = jnp.where((source_of == order[0]) | (receiver == order[0]) | (sizes[receiver] == 0), 0, jnp.maximum(margin, 0))
    moved = jax.random.randint(jax.random.fold_in(own, 4), (amount // 2,), 0, 1 << 20) % (margin + 1)
    sizes = sizes.at[source_of].add(-moved).at[receiver].add(moved)
    members = jnp.searchsorted(jnp.cumsum(sizes), jnp.arange(rows * top), side="right").astype(jnp.int32)
    listing = members.reshape(top, rows).T
    listing = listing[jax.random.permutation(jax.random.fold_in(own, 1), rows)]
    rotation = jax.random.randint(jax.random.fold_in(own, 2), (rows, 1), 0, top)
    return jnp.take_along_axis(listing, (jnp.arange(top)[None, :] + rotation) % top, axis=1)


def load_shares(number_of, total, most, lean, full):
    portions = [(1 << 20) // math.isqrt(rank ** lean) + 1 for rank in range(1, number_of + 1)]
    largest = most if full else min(most, max(-(-total // number_of), total * portions[0] // sum(portions)))
    least = 1 if total - largest >= number_of - 1 else 0
    given, surplus = [largest] + [least] * (number_of - 1), total - largest - least * (number_of - 1)
    while surplus > 0:
        candidates = [i for i in range(1, number_of) if given[i] < largest] or [i for i in range(1, number_of) if given[i] < most]
        pool, left = sum([portions[i] for i in candidates]), surplus
        for i in candidates:
            extra = min(most - given[i], max(1, left * portions[i] // pool), surplus)
            given[i] = given[i] + extra
            surplus = surplus - extra
    return np.array(given)


def bell_draw(stream_key, shape, scale, limit, split=(), kind=jnp.bfloat16):
    drawn = scale * jax.random.normal(stream_key, shape, jnp.float32)
    if split:
        drawn = drawn * levels(stream_key, shape, split, -0.22, 0.18)
    return jnp.clip(drawn, -limit, limit).astype(kind)


def setup_inputs(seed: int = 0) -> dict:
    streams_of = jax.random.split(jax.random.key(seed), 5)
    coregistered_sweeps = bell_draw(streams_of[0], (N_PAIR, N_GROUND, SWEEP_HEIGHT, 2, SWEEP_WIDTH), 1.0, 6.0, ((0, 2), (1, 16)))
    shard_opening_height = plant(jax.random.randint(streams_of[1], (SHARD_OVERALL,), 0, SWEEP_HEIGHT - SHARD_HEIGHT + 1), jax.random.fold_in(streams_of[1], 1), 0, SWEEP_HEIGHT - SHARD_HEIGHT).astype(jnp.int32)
    shard_goal_patch_keys = jax.random.split(jax.random.fold_in(streams_of[2], 1), SHARD_OVERALL // PIECE_DEV)
    shard_goal_patch_turns = jax.random.permutation(jax.random.fold_in(streams_of[2], 3), SHARD_OVERALL // PIECE_DEV)
    shard_goal_patch = jax.vmap(lambda own, number: assign_block(jax.random.fold_in(streams_of[2], 2), own, number, PIECE_DEV, N_GROUND, 1, CAP, 2))(shard_goal_patch_keys, shard_goal_patch_turns).reshape((SHARD_OVERALL, 1))
    shard_patch_place = plant(jax.random.randint(streams_of[3], (SHARD_OVERALL,), 0, SLOTS), jax.random.fold_in(streams_of[3], 1), 0, SLOTS - 1).astype(jnp.int32)
    return {"coregistered_sweeps": coregistered_sweeps, "shard_opening_height": shard_opening_height, "shard_goal_patch": shard_goal_patch, "shard_patch_place": shard_patch_place}


def multilook(reference_tiles, secondary_tiles):
    first = reference_tiles.astype(jnp.float32)
    second = secondary_tiles.astype(jnp.float32)
    real_part = first[..., 0, :] * second[..., 0, :] + first[..., 1, :] * second[..., 1, :]
    imag_part = first[..., 1, :] * second[..., 0, :] - first[..., 0, :] * second[..., 1, :]
    joined = jnp.stack([real_part, imag_part], axis=-3)
    leading = joined.shape[:-2]
    row_count = joined.shape[-2]
    col_count = joined.shape[-1]
    boxes = joined.reshape(leading + (row_count // LOOK_ROWS, LOOK_ROWS, col_count // LOOK_COLS, LOOK_COLS))
    return jnp.mean(boxes, axis=(-3, -1))


def goldstein(looked):
    field = looked[..., 0, :, :] + 1j * looked[..., 1, :, :]
    spectrum = jnp.fft.fft2(field)
    weight = (spectrum.real ** 2 + spectrum.imag ** 2 + 1e-6) ** 0.25
    weight = weight / jnp.mean(weight, axis=(-2, -1), keepdims=True)
    result = jnp.fft.ifft2(spectrum * weight)
    return jnp.stack([result.real, result.imag], axis=-3).astype(jnp.float32)


def reference(coregistered_sweeps, shard_opening_height, shard_goal_patch, shard_patch_place):
    provider = (jnp.arange(SHARD_OVERALL) // PIECE_DEV).astype(jnp.int32)
    sweep_height_offset = shard_opening_height[:, None] + jnp.arange(SHARD_HEIGHT, dtype=jnp.int32)[None, :]
    slot_key = shard_goal_patch[:, 0] * SLOTS + shard_patch_place
    counts = jax.ops.segment_sum(jnp.ones((SHARD_OVERALL,), jnp.float32), slot_key, num_segments=N_GROUND * SLOTS)
    divisor = jnp.maximum(counts, 1.0)

    def compose_earth_patches(radar_pass):
        shards = radar_pass[provider[:, None], sweep_height_offset].astype(jnp.float32)
        totals = jax.ops.segment_sum(shards, slot_key, num_segments=N_GROUND * SLOTS)
        smoothed_pixel_mean = (totals / divisor[:, None, None, None]).astype(jnp.bfloat16)
        refolded_patches = smoothed_pixel_mean.reshape(N_GROUND, PATCH_SHARD_LEVEL, 2, SHARD_HEIGHT, 2, SWEEP_WIDTH)
        return refolded_patches.transpose(0, 1, 3, 4, 2, 5).reshape(N_GROUND, TILE_ROWS, 2, TILE_COLS)

    earth_patch_pile = lax.map(compose_earth_patches, coregistered_sweeps)

    def per_acquisition(index):
        secondary = earth_patch_pile[index]
        order = jnp.arange(PAIR_DEV, dtype=jnp.int32)
        partners = (order + (order >= index).astype(jnp.int32)).astype(jnp.int32)

        def per_pair(other):
            return goldstein(multilook(earth_patch_pile[other], secondary))

        return lax.map(per_pair, partners)

    return lax.map(per_acquisition, jnp.arange(N_PAIR, dtype=jnp.int32))
```

```python
import functools
import math

import jax
import jax.numpy as jnp
import numpy as np
from jax import lax
from jax.experimental import pallas as pl
from jax.experimental.pallas import tpu as pltpu
from jax.sharding import PartitionSpec as P

LOOK_ROWS = 4
LOOK_COLS = 16
SHARD_HEIGHT = 16
TILE_ROWS = 256
TILE_COLS = 1024
SWEEP_WIDTH = 512
PATCH_SHARD_LEVEL = 16
SLOTS = 32


def multilook(reference_tiles, secondary_tiles):
    first = reference_tiles.astype(jnp.float32)
    second = secondary_tiles.astype(jnp.float32)
    real_part = first[..., 0, :] * second[..., 0, :] + first[..., 1, :] * second[..., 1, :]
    imag_part = first[..., 1, :] * second[..., 0, :] - first[..., 0, :] * second[..., 1, :]
    joined = jnp.stack([real_part, imag_part], axis=-3)
    leading = joined.shape[:-2]
    row_count = joined.shape[-2]
    col_count = joined.shape[-1]
    boxes = joined.reshape(
        leading + (row_count // LOOK_ROWS, LOOK_ROWS, col_count // LOOK_COLS, LOOK_COLS)
    )
    return jnp.mean(boxes, axis=(-3, -1))


def on_left(matrix, field):
    return jnp.einsum("ij,...jk->...ik", matrix, field, precision=lax.Precision.HIGHEST)


def on_right(field, matrix):
    return jnp.einsum("...ij,jk->...ik", field, matrix, precision=lax.Precision.HIGHEST)


def goldstein(looked):
    length = looked.shape[-1]
    positions = jnp.arange(length, dtype=jnp.int32)
    phase = positions[:, None] * positions[None, :] % length
    angle = phase.astype(jnp.float32) * (2.0 * math.pi / length)
    cosine = jnp.cos(angle)
    sine = jnp.sin(angle)
    real_in = looked[..., 0, :, :]
    imag_in = looked[..., 1, :, :]
    half_real = on_left(cosine, real_in) + on_left(sine, imag_in)
    half_imag = on_left(cosine, imag_in) - on_left(sine, real_in)
    spec_real = on_right(half_real, cosine) + on_right(half_imag, sine)
    spec_imag = on_right(half_imag, cosine) - on_right(half_real, sine)
    weight = (spec_real * spec_real + spec_imag * spec_imag + 1e-06) ** 0.25
    weight = weight / jnp.mean(weight, axis=(-2, -1), keepdims=True)
    spec_real = spec_real * weight
    spec_imag = spec_imag * weight
    back_real = on_left(cosine, spec_real) - on_left(sine, spec_imag)
    back_imag = on_left(cosine, spec_imag) + on_left(sine, spec_real)
    out_real = on_right(back_real, cosine) - on_right(back_imag, sine)
    out_imag = on_right(back_imag, cosine) + on_right(back_real, sine)
    scale = 1.0 / (length * length)
    return jnp.stack([out_real * scale, out_imag * scale], axis=-3)


def partners_of(index, pair_width):
    order = jnp.arange(pair_width, dtype=jnp.int32)
    return order + (order >= index).astype(jnp.int32)


def local(coregistered_sweeps, shard_opening_height, shard_goal_patch, shard_patch_place):
    earth_patch_total_size = lax.axis_size("ground")
    pair_count = lax.axis_size("pair")
    piece_count = shard_opening_height.shape[0]
    place_allowance = max(
        2, (2 * piece_count + earth_patch_total_size - 1) // earth_patch_total_size
    )
    sweep_resident = coregistered_sweeps[0, 0]
    target = shard_goal_patch[:, 0]
    hits = (target[:, None] == jnp.arange(earth_patch_total_size, dtype=jnp.int32)[None, :]).astype(
        jnp.int32
    )
    earlier = jnp.cumsum(hits, axis=0) - hits
    rank = jnp.sum(earlier * hits, axis=1)
    position = target * place_allowance + rank
    matches = (
        position[None, :]
        == jnp.arange(earth_patch_total_size * place_allowance, dtype=jnp.int32)[:, None]
    ).astype(jnp.int32)
    tiles_filled = jnp.sum(matches, axis=1) > 0
    chosen = jnp.sum(matches * jnp.arange(piece_count, dtype=jnp.int32)[None, :], axis=1)
    sweep_height_offset = (
        shard_opening_height[chosen][:, None] + jnp.arange(SHARD_HEIGHT, dtype=jnp.int32)[None, :]
    )
    pieces_to_send = jnp.where(
        tiles_filled[:, None, None, None],
        sweep_resident[sweep_height_offset],
        jnp.zeros((), jnp.bfloat16),
    )
    labels = jnp.where(tiles_filled, shard_patch_place[chosen] + 1, 0).astype(jnp.bfloat16)
    received_pieces, arrived_labels = (
        lax.all_to_all(
            pieces_to_send.reshape(
                earth_patch_total_size, place_allowance, SHARD_HEIGHT, 2, SWEEP_WIDTH
            ),
            "ground",
            split_axis=0,
            concat_axis=0,
            tiled=True,
        ),
        lax.all_to_all(
            labels.reshape(earth_patch_total_size, place_allowance),
            "ground",
            split_axis=0,
            concat_axis=0,
            tiled=True,
        ),
    )
    pieces_flattened = received_pieces.reshape(
        earth_patch_total_size * place_allowance, SHARD_HEIGHT * 2 * SWEEP_WIDTH
    )
    slot_labels = (jnp.arange(SLOTS, dtype=jnp.int32) + 1).astype(jnp.bfloat16)
    selector = arrived_labels.reshape(-1)[None, :] == slot_labels[:, None]
    totals = jnp.dot(
        selector.astype(jnp.bfloat16), pieces_flattened, preferred_element_type=jnp.float32
    )
    counts = jnp.sum(selector.astype(jnp.float32), axis=1)
    smoothed_pixel_mean = (totals / jnp.maximum(counts, 1.0)[:, None]).astype(jnp.bfloat16)
    ground_tile = (
        smoothed_pixel_mean.reshape(PATCH_SHARD_LEVEL, 2, SHARD_HEIGHT, 2, SWEEP_WIDTH)
        .transpose(0, 2, 3, 1, 4)
        .reshape(TILE_ROWS, 2, TILE_COLS)
    )
    pair_width = pair_count - 1
    own_refs = partners_of(lax.axis_index("pair"), pair_width)
    piece = lax.all_gather(ground_tile[None], "pair", axis=0, tiled=True)
    looked_piece = multilook(piece, ground_tile[None])
    indices = jnp.arange(piece.shape[0], dtype=jnp.int32)
    selection = (own_refs[:, None] == indices[None, :]).astype(jnp.float32)
    looked = jnp.einsum("kn,nabc->kabc", selection, looked_piece, precision=lax.Precision.HIGHEST)
    return goldstein(looked)[None, :, None]


def general(mesh):
    placed = (P("pair", "ground", None, None, None), P("ground"), P("ground", None), P("ground"))
    return jax.shard_map(
        local,
        mesh=mesh,
        in_specs=placed,
        out_specs=P("pair", None, "ground", None, None, None),
        check_vma=False,
    )


CAP_VMEM = 48 * 1024 * 1024
MESH = pl.DeviceIdType.MESH
EXACT = lax.Precision.HIGHEST


def table_kernel(allowance, opening, goal, place, starts, labels):
    tile_count = starts.shape[0]
    for tile in range(tile_count):
        for slot in range(allowance):
            starts[tile, slot] = 0
            labels[tile, 0, slot] = 0

    def clear(tile, carry):
        labels[tile, 0, allowance] = 0
        return carry

    lax.fori_loop(0, tile_count, clear, 0)

    def enter(piece, carry):
        tile = goal[piece]
        rank = labels[tile, 0, allowance]
        starts[tile, rank] = opening[piece]
        labels[tile, 0, rank] = place[piece] + 1
        labels[tile, 0, allowance] = rank + 1
        return carry

    lax.fori_loop(0, opening.shape[0], enter, 0)


def exchange_kernel(
    tile_count, allowance, starts, labels, sweep, arrived, arrived_labels,
    outgoing, send_sem, recv_sem, label_send, label_recv, own_sem,
):
    me = lax.axis_index("ground")
    mine = lax.axis_index("pair")
    half = SHARD_HEIGHT // 2
    barrier = pltpu.get_barrier_semaphore()

    def greet(step, carry):
        pl.semaphore_signal(
            barrier, inc=1,
            device_id={"ground": lax.rem(me + step // 2, tile_count), "pair": lax.rem(mine + step, 2)},
            device_id_type=MESH,
        )
        return carry

    lax.fori_loop(1, 2 * tile_count, greet, 0)

    def extract(tile):
        def one(slot, carry):
            top = starts[tile, slot]
            outgoing[tile, 0, pl.ds(slot * half, half)] = sweep[pl.ds(top, half)]
            outgoing[tile, 1, pl.ds(slot * half, half)] = sweep[pl.ds(top + half, half)]
            return carry

        lax.fori_loop(0, allowance, one, 0)

    def parcel(tile, other, source, source_pair):
        return pltpu.make_async_remote_copy(
            src_ref=outgoing.at[tile, other],
            dst_ref=arrived.at[source_pair, source],
            send_sem=send_sem.at[tile, other],
            recv_sem=recv_sem.at[source_pair, source],
            device_id={"ground": tile, "pair": other},
            device_id_type=MESH,
        )

    def tag(tile, source):
        return pltpu.make_async_remote_copy(
            src_ref=labels.at[tile],
            dst_ref=arrived_labels.at[source],
            send_sem=label_send.at[tile],
            recv_sem=label_recv.at[source],
            device_id={"ground": tile, "pair": mine},
            device_id_type=MESH,
        )

    def target_of(step):
        return lax.rem(me + step, tile_count)

    first = target_of(tile_count // 2)
    extract(first)
    pl.semaphore_wait(barrier, 2 * tile_count - 1)

    def send(tile):
        parcel(tile, 1 - mine, me, mine).start()
        parcel(tile, mine, me, mine).start()
        tag(tile, me).start()

    send(first)

    def pairs(step, carry):
        tile = target_of(tile_count // 2 + step)
        extract(tile)
        send(tile)
        tile = target_of(tile_count // 2 - step)
        extract(tile)
        send(tile)
        return carry

    lax.fori_loop(1, tile_count // 2, pairs, 0)
    extract(me)
    parcel(me, 1 - mine, me, mine).start()
    own = pltpu.make_async_copy(outgoing.at[me, mine], arrived.at[mine, me], own_sem.at[0])
    own.start()
    own_tag = pltpu.make_async_copy(labels.at[me], arrived_labels.at[me], own_sem.at[1])
    own_tag.start()

    def finish(step, carry):
        tile = target_of(step)
        parcel(tile, 1 - mine, tile, 1 - mine).wait_recv()
        parcel(tile, mine, tile, mine).wait_recv()
        tag(tile, tile).wait_recv()
        parcel(tile, 1 - mine, me, mine).wait_send()
        parcel(tile, mine, me, mine).wait_send()
        tag(tile, me).wait_send()
        return carry

    lax.fori_loop(1, tile_count, finish, 0)
    parcel(me, 1 - mine, me, 1 - mine).wait_recv()
    parcel(me, 1 - mine, me, mine).wait_send()
    own.wait()
    own_tag.wait()


def combine_kernel(allowance, labels, arrived, spread, mask, gather, looked, total, count, prods):
    source = pl.program_id(0)
    half = SHARD_HEIGHT // 2

    @pl.when(source == 0)
    def _():
        total[...] = jnp.zeros_like(total)
        for slot in range(SLOTS):
            count[slot] = 0

    for slot in range(allowance):
        label = labels[source, 0, slot]

        @pl.when(label > 0)
        def _():
            count[label - 1] = count[label - 1] + 1
            for part in range(2):
                total[part, label - 1] += arrived[part, 0, pl.ds(slot * half, half)].astype(jnp.float32)

    @pl.when(source == pl.num_programs(0) - 1)
    def _():
        def one(level, carry):
            for side in range(2):
                slot = level * 2 + side
                divisor = jnp.maximum(count[slot], 1).astype(jnp.float32)
                first = (total[1, slot] / divisor).astype(jnp.bfloat16).astype(jnp.float32)
                second = (total[0, slot] / divisor).astype(jnp.bfloat16).astype(jnp.float32)
                same = first * second
                cross = first * jnp.concatenate([second[:, 4:], second[:, :4]], axis=1)
                for box in range(2):
                    rows = slice(box * LOOK_ROWS, (box + 1) * LOOK_ROWS)
                    at = pl.ds(pl.multiple_of((level * 2 + box) * 8, 8), 8)
                    prods[side, 0, at, :] = jnp.sum(same[rows], axis=0)
                    prods[side, 1, at, :] = jnp.sum(cross[rows], axis=0)
            return carry

        lax.fori_loop(0, PATCH_SHARD_LEVEL, one, 0)
        pooled = jnp.zeros(mask.shape[1:], jnp.float32)
        for side in range(2):
            wide = jnp.dot(prods[side, 0], spread[0], precision=EXACT, preferred_element_type=jnp.float32)
            wide += jnp.dot(prods[side, 1], spread[1], precision=EXACT, preferred_element_type=jnp.float32)
            pooled += wide * mask[side]
        looked[...] = jnp.dot(gather[...], pooled, precision=EXACT, preferred_element_type=jnp.float32)


def filter_kernel(looked, place, left, right, right_back, out, other, send_sem, recv_sem):
    mine = lax.axis_index("pair")
    barrier = pltpu.get_barrier_semaphore()
    pl.semaphore_signal(barrier, inc=1, device_id={"pair": 1 - mine}, device_id_type=MESH)
    pl.semaphore_wait(barrier, 1)
    copy = pltpu.make_async_remote_copy(
        src_ref=looked, dst_ref=other, send_sem=send_sem, recv_sem=recv_sem,
        device_id={"pair": 1 - mine}, device_id_type=MESH,
    )
    copy.start()

    def dot(a, b):
        return jnp.dot(a, b, precision=EXACT, preferred_element_type=jnp.float32)

    length = left.shape[1]
    lane = lax.broadcasted_iota(jnp.int32, (length, 2 * length), 1)
    turn = jnp.where(lane < length, 1.0, -1.0)
    flip = jnp.where(lane < length, 1.0, 1.0 - 2.0 * mine.astype(jnp.float32))
    own = dot(place[mine], looked[...])
    copy.wait()
    field = (own + dot(place[1 - mine], other[...])) * flip
    both = dot(left[...], field)
    spectrum = both[:length] + turn * pltpu.roll(both[length:], length, 1)
    spectrum = dot(spectrum, right[...])
    power = spectrum * spectrum
    power = power + pltpu.roll(power, length, 1)
    weight = jnp.sqrt(jnp.sqrt(power + 1e-06))
    mean = jnp.sum(weight) * (1.0 / (2 * length * length))
    spectrum = spectrum * (weight / mean)
    both = dot(left[...], spectrum)
    back = both[:length] - turn * pltpu.roll(both[length:], length, 1)
    back = dot(back, right_back[...]) * (1.0 / (length * length))
    out[0] = back[:, :length]
    out[1] = back[:, length:]


def constants():
    lane = np.arange(128)
    column = np.arange(64)
    pick = (lane[:, None] // LOOK_COLS == column[None, :] % 8).astype(np.float32)
    nil = np.zeros_like(pick)
    spread = np.stack([np.concatenate([pick, nil], 1), np.concatenate([nil, pick], 1)])
    sub = np.arange(256) % 8
    masks = []
    for side in range(2):
        hit = (column[None, :] // 8 == side * 4 + sub[:, None] % 4).astype(np.float32)
        sign = np.where(sub[:, None] < 4, -1.0, 1.0).astype(np.float32)
        masks.append(np.concatenate([hit, hit * sign], 1))
    mask = np.stack(masks)
    gather = (np.arange(32)[:, None] == np.arange(256)[None, :] // 8).astype(np.float32)
    gather = gather / (LOOK_ROWS * LOOK_COLS)
    row = np.arange(32)
    place = np.zeros((2, 64, 32), np.float32)
    for pair in range(2):
        place[pair, 4 * (row // 2) + 2 * pair + row % 2, row] = 1.0
    angle = (column[:, None] * column[None, :] % 64) * (2.0 * math.pi / 64)
    cosine, sine = np.cos(angle), np.sin(angle)
    left = np.concatenate([cosine, sine], 0)
    right = np.block([[cosine, -sine], [sine, cosine]])
    right_back = np.block([[cosine, sine], [-sine, cosine]])
    return (spread, mask, gather), tuple(x.astype(np.float32) for x in (place, left, right, right_back))


def local_pair(coregistered_sweeps, shard_opening_height, shard_goal_patch, shard_patch_place):
    tile_count = lax.axis_size("ground")
    piece_count = shard_opening_height.shape[0]
    allowance = max(2, (2 * piece_count + tile_count - 1) // tile_count)
    half = SHARD_HEIGHT // 2
    pool, transforms = constants()
    smem = pl.BlockSpec(memory_space=pltpu.SMEM)
    vmem = pl.BlockSpec(memory_space=pltpu.VMEM)
    anyplace = pl.BlockSpec(memory_space=pl.ANY)
    starts, labels = pl.pallas_call(
        functools.partial(table_kernel, allowance),
        out_shape=(
            jax.ShapeDtypeStruct((tile_count, allowance), jnp.int32),
            jax.ShapeDtypeStruct((tile_count, 1, 128), jnp.int32),
        ),
        in_specs=[smem] * 3,
        out_specs=(smem, smem),
    )(shard_opening_height, shard_goal_patch[:, 0], shard_patch_place)
    sweep = coregistered_sweeps[0, 0].reshape(-1, 8, 128)
    arrived, arrived_labels = pl.pallas_call(
        functools.partial(exchange_kernel, tile_count, allowance),
        out_shape=(
            jax.ShapeDtypeStruct((2, tile_count, allowance * half, 8, 128), jnp.bfloat16),
            jax.ShapeDtypeStruct((tile_count, 1, 128), jnp.int32),
        ),
        in_specs=[smem, vmem, vmem],
        out_specs=(anyplace, vmem),
        scratch_shapes=[
            pltpu.VMEM((tile_count, 2, allowance * half, 8, 128), jnp.bfloat16),
            pltpu.SemaphoreType.DMA((tile_count, 2)),
            pltpu.SemaphoreType.DMA((2, tile_count)),
            pltpu.SemaphoreType.DMA((tile_count,)),
            pltpu.SemaphoreType.DMA((tile_count,)),
            pltpu.SemaphoreType.DMA((2,)),
        ],
        compiler_params=pltpu.CompilerParams(
            collective_id=0, has_side_effects=True, vmem_limit_bytes=CAP_VMEM
        ),
    )(starts, labels, sweep)
    looked = pl.pallas_call(
        functools.partial(combine_kernel, allowance),
        grid=(tile_count,),
        out_shape=jax.ShapeDtypeStruct((32, 128), jnp.float32),
        in_specs=[
            smem,
            pl.BlockSpec((2, 1, allowance * half, 8, 128), lambda i: (0, i, 0, 0, 0)),
            vmem, vmem, vmem,
        ],
        out_specs=vmem,
        scratch_shapes=[
            pltpu.VMEM((2, SLOTS, half, 8, 128), jnp.float32),
            pltpu.SMEM((SLOTS,), jnp.int32),
            pltpu.VMEM((2, 2, 256, 128), jnp.float32),
        ],
        compiler_params=pltpu.CompilerParams(vmem_limit_bytes=CAP_VMEM),
    )(arrived_labels, arrived, *pool)
    filtered = pl.pallas_call(
        filter_kernel,
        out_shape=jax.ShapeDtypeStruct((2, 64, 64), jnp.float32),
        in_specs=[vmem] * 5,
        out_specs=vmem,
        scratch_shapes=[
            pltpu.VMEM((32, 128), jnp.float32),
            pltpu.SemaphoreType.DMA,
            pltpu.SemaphoreType.DMA,
        ],
        compiler_params=pltpu.CompilerParams(collective_id=1, has_side_effects=True),
    )(looked, *transforms)
    return filtered[None, None, None]


def solution(mesh):
    if mesh.shape["pair"] != 2:
        return general(mesh)
    placed = (P("pair", "ground", None, None, None), P("ground"), P("ground", None), P("ground"))
    return jax.shard_map(
        local_pair,
        mesh=mesh,
        in_specs=placed,
        out_specs=P("pair", None, "ground", None, None, None),
        check_vma=False,
    )
```

```python
import functools
import math

import jax
import jax.numpy as jnp
import numpy as np
from jax import lax
from jax.experimental import pallas as pl
from jax.experimental.pallas import tpu as pltpu
from jax.sharding import PartitionSpec as P

LOOK_ROWS = 4
LOOK_COLS = 16
SHARD_HEIGHT = 16
TILE_ROWS = 256
TILE_COLS = 1024
SWEEP_WIDTH = 512
PATCH_SHARD_LEVEL = 16
SLOTS = 32


def multilook(reference_tiles, secondary_tiles):
    first = reference_tiles.astype(jnp.float32)
    second = secondary_tiles.astype(jnp.float32)
    real_part = first[..., 0, :] * second[..., 0, :] + first[..., 1, :] * second[..., 1, :]
    imag_part = first[..., 1, :] * second[..., 0, :] - first[..., 0, :] * second[..., 1, :]
    joined = jnp.stack([real_part, imag_part], axis=-3)
    leading = joined.shape[:-2]
    row_count = joined.shape[-2]
    col_count = joined.shape[-1]
    boxes = joined.reshape(
        leading + (row_count // LOOK_ROWS, LOOK_ROWS, col_count // LOOK_COLS, LOOK_COLS)
    )
    return jnp.mean(boxes, axis=(-3, -1))


def on_left(matrix, field):
    return jnp.einsum("ij,...jk->...ik", matrix, field, precision=lax.Precision.HIGHEST)


def on_right(field, matrix):
    return jnp.einsum("...ij,jk->...ik", field, matrix, precision=lax.Precision.HIGHEST)


def goldstein(looked):
    length = looked.shape[-1]
    positions = jnp.arange(length, dtype=jnp.int32)
    phase = positions[:, None] * positions[None, :] % length
    angle = phase.astype(jnp.float32) * (2.0 * math.pi / length)
    cosine = jnp.cos(angle)
    sine = jnp.sin(angle)
    real_in = looked[..., 0, :, :]
    imag_in = looked[..., 1, :, :]
    half_real = on_left(cosine, real_in) + on_left(sine, imag_in)
    half_imag = on_left(cosine, imag_in) - on_left(sine, real_in)
    spec_real = on_right(half_real, cosine) + on_right(half_imag, sine)
    spec_imag = on_right(half_imag, cosine) - on_right(half_real, sine)
    weight = (spec_real * spec_real + spec_imag * spec_imag + 1e-06) ** 0.25
    weight = weight / jnp.mean(weight, axis=(-2, -1), keepdims=True)
    spec_real = spec_real * weight
    spec_imag = spec_imag * weight
    back_real = on_left(cosine, spec_real) - on_left(sine, spec_imag)
    back_imag = on_left(cosine, spec_imag) + on_left(sine, spec_real)
    out_real = on_right(back_real, cosine) - on_right(back_imag, sine)
    out_imag = on_right(back_imag, cosine) + on_right(back_real, sine)
    scale = 1.0 / (length * length)
    return jnp.stack([out_real * scale, out_imag * scale], axis=-3)


def partners_of(index, pair_width):
    order = jnp.arange(pair_width, dtype=jnp.int32)
    return order + (order >= index).astype(jnp.int32)


def local(coregistered_sweeps, shard_opening_height, shard_goal_patch, shard_patch_place):
    earth_patch_total_size = lax.axis_size("ground")
    pair_count = lax.axis_size("pair")
    piece_count = shard_opening_height.shape[0]
    place_allowance = max(
        2, (2 * piece_count + earth_patch_total_size - 1) // earth_patch_total_size
    )
    sweep_resident = coregistered_sweeps[0, 0]
    target = shard_goal_patch[:, 0]
    hits = (target[:, None] == jnp.arange(earth_patch_total_size, dtype=jnp.int32)[None, :]).astype(
        jnp.int32
    )
    earlier = jnp.cumsum(hits, axis=0) - hits
    rank = jnp.sum(earlier * hits, axis=1)
    position = target * place_allowance + rank
    matches = (
        position[None, :]
        == jnp.arange(earth_patch_total_size * place_allowance, dtype=jnp.int32)[:, None]
    ).astype(jnp.int32)
    tiles_filled = jnp.sum(matches, axis=1) > 0
    chosen = jnp.sum(matches * jnp.arange(piece_count, dtype=jnp.int32)[None, :], axis=1)
    sweep_height_offset = (
        shard_opening_height[chosen][:, None] + jnp.arange(SHARD_HEIGHT, dtype=jnp.int32)[None, :]
    )
    pieces_to_send = jnp.where(
        tiles_filled[:, None, None, None],
        sweep_resident[sweep_height_offset],
        jnp.zeros((), jnp.bfloat16),
    )
    labels = jnp.where(tiles_filled, shard_patch_place[chosen] + 1, 0).astype(jnp.bfloat16)
    received_pieces, arrived_labels = (
        lax.all_to_all(
            pieces_to_send.reshape(
                earth_patch_total_size, place_allowance, SHARD_HEIGHT, 2, SWEEP_WIDTH
            ),
            "ground",
            split_axis=0,
            concat_axis=0,
            tiled=True,
        ),
        lax.all_to_all(
            labels.reshape(earth_patch_total_size, place_allowance),
            "ground",
            split_axis=0,
            concat_axis=0,
            tiled=True,
        ),
    )
    pieces_flattened = received_pieces.reshape(
        earth_patch_total_size * place_allowance, SHARD_HEIGHT * 2 * SWEEP_WIDTH
    )
    slot_labels = (jnp.arange(SLOTS, dtype=jnp.int32) + 1).astype(jnp.bfloat16)
    selector = arrived_labels.reshape(-1)[None, :] == slot_labels[:, None]
    totals = jnp.dot(
        selector.astype(jnp.bfloat16), pieces_flattened, preferred_element_type=jnp.float32
    )
    counts = jnp.sum(selector.astype(jnp.float32), axis=1)
    smoothed_pixel_mean = (totals / jnp.maximum(counts, 1.0)[:, None]).astype(jnp.bfloat16)
    ground_tile = (
        smoothed_pixel_mean.reshape(PATCH_SHARD_LEVEL, 2, SHARD_HEIGHT, 2, SWEEP_WIDTH)
        .transpose(0, 2, 3, 1, 4)
        .reshape(TILE_ROWS, 2, TILE_COLS)
    )
    pair_width = pair_count - 1
    own_refs = partners_of(lax.axis_index("pair"), pair_width)
    piece = lax.all_gather(ground_tile[None], "pair", axis=0, tiled=True)
    looked_piece = multilook(piece, ground_tile[None])
    indices = jnp.arange(piece.shape[0], dtype=jnp.int32)
    selection = (own_refs[:, None] == indices[None, :]).astype(jnp.float32)
    looked = jnp.einsum("kn,nabc->kabc", selection, looked_piece, precision=lax.Precision.HIGHEST)
    return goldstein(looked)[None, :, None]


def general(mesh):
    placed = (P("pair", "ground", None, None, None), P("ground"), P("ground", None), P("ground"))
    return jax.shard_map(
        local,
        mesh=mesh,
        in_specs=placed,
        out_specs=P("pair", None, "ground", None, None, None),
        check_vma=False,
    )


CHUNKS = 2
MESH = pl.DeviceIdType.MESH
EXACT = lax.Precision.HIGHEST


def table_kernel(allowance, opening, goal, place, starts, labels):
    tile_count = starts.shape[0]

    def clear(tile, carry):
        for slot in range(allowance):
            starts[tile, slot] = 0
            labels[tile, 0, slot] = 0
            labels[tile, 0, 2 * allowance + slot] = 0
        labels[tile, 0, allowance] = 0
        return carry

    lax.fori_loop(0, tile_count, clear, 0)

    def enter(piece, carry):
        tile = goal[piece]
        rank = labels[tile, 0, allowance]
        starts[tile, rank] = opening[piece]
        labels[tile, 0, rank] = place[piece] + 1
        labels[tile, 0, 2 * allowance + rank] = opening[piece]
        labels[tile, 0, allowance] = rank + 1
        return carry

    lax.fori_loop(0, opening.shape[0], enter, 0)


def exchange_kernel(
    allowance, starts, labels, sweep, arrived, relayed, arrived_labels,
    outgoing, send_sem, recv_sem, label_send, label_recv, own_sem,
    burst_send, relay_send, relay_recv,
):
    me = lax.axis_index("ground")
    mine = lax.axis_index("pair")
    tile_count = 16
    level = me // 4
    line = lax.rem(me, 4)
    across = lax.rem(line + 2, 4)
    beside = line + 1 - 2 * lax.rem(line, 2)
    across_beside = lax.rem(beside + 2, 4)
    inner = jnp.logical_or(level == 1, level == 2)
    right = level // 2
    outward = 3 * right
    far = 2 - right
    barrier = pltpu.get_barrier_semaphore()

    def greet(step, carry):
        pl.semaphore_signal(
            barrier, inc=1,
            device_id={"ground": lax.rem(me + step // 2, tile_count), "pair": lax.rem(mine + step, 2)},
            device_id_type=MESH,
        )
        return carry

    lax.fori_loop(1, 2 * tile_count, greet, 0)

    def extract(tile):
        def one(slot, carry):
            top = starts[tile, slot]
            for part in range(2):
                outgoing[tile, part, pl.ds(slot * SHARD_HEIGHT, SHARD_HEIGHT)] = sweep[
                    part, pl.ds(top, SHARD_HEIGHT)
                ]
            return carry

        lax.fori_loop(0, allowance, one, 0)

    def parcel(tile, other, source, source_pair):
        return pltpu.make_async_remote_copy(
            src_ref=outgoing.at[tile, other],
            dst_ref=arrived.at[source_pair, source],
            send_sem=send_sem.at[tile, other],
            recv_sem=recv_sem.at[source_pair, source],
            device_id={"ground": tile, "pair": other},
            device_id_type=MESH,
        )

    def tag(tile, source):
        return pltpu.make_async_remote_copy(
            src_ref=labels.at[tile],
            dst_ref=arrived_labels.at[source],
            send_sem=label_send.at[tile],
            recv_sem=label_recv.at[source],
            device_id={"ground": tile, "pair": mine},
            device_id_type=MESH,
        )

    span = sweep.shape[1] // CHUNKS

    def burst(part, chunk):
        rows = pl.ds(chunk * span, span)
        return pltpu.make_async_remote_copy(
            src_ref=sweep.at[part, rows],
            dst_ref=relayed.at[line, mine, rows],
            send_sem=burst_send.at[part, chunk],
            recv_sem=relay_recv.at[line, mine, chunk],
            device_id={"ground": far * 4 + line, "pair": part},
            device_id_type=MESH,
        )

    def relay(kind, which, target, pair, chunk):
        rows = pl.ds(chunk * span, span)
        return pltpu.make_async_remote_copy(
            src_ref=relayed.at[which, pair, rows],
            dst_ref=relayed.at[which, pair, rows],
            send_sem=relay_send.at[kind, pair, chunk],
            recv_sem=relay_recv.at[which, pair, chunk],
            device_id={"ground": target, "pair": mine},
            device_id_type=MESH,
        )

    def target_of(step):
        return lax.rem(me + step, tile_count)

    def takes(tile):
        return jnp.logical_or(jnp.logical_not(inner), tile // 8 == right)

    def send(tile):
        tag(tile, me).start()

        @pl.when(takes(tile))
        def _():
            extract(tile)
            parcel(tile, 1 - mine, me, mine).start()
            parcel(tile, mine, me, mine).start()

    pl.semaphore_wait(barrier, 2 * tile_count - 1)

    @pl.when(inner)
    def _():
        for chunk in range(CHUNKS):
            for part in range(2):
                burst(part, chunk).start()

    send(target_of(tile_count // 2))

    def pairs(step, carry):
        send(target_of(tile_count // 2 + step))
        send(target_of(tile_count // 2 - step))
        return carry

    lax.fori_loop(1, tile_count // 2, pairs, 0)
    extract(me)
    parcel(me, 1 - mine, me, mine).start()
    own = pltpu.make_async_copy(outgoing.at[me, mine], arrived.at[mine, me], own_sem.at[0])
    own.start()
    own_tag = pltpu.make_async_copy(labels.at[me], arrived_labels.at[me], own_sem.at[1])
    own_tag.start()

    base = level * 4
    order = [(pair, chunk) for chunk in range(CHUNKS) for pair in range(2)]

    def second(pair, chunk):
        relay(1, across, base + across, pair, chunk).wait_recv()
        relay(3, across, base + beside, pair, chunk).start()

    for spot, (pair, chunk) in enumerate(order):
        relay(0, line, base + across, pair, chunk).wait_recv()

        @pl.when(inner)
        def _():
            relay(0, line, outward * 4 + line, pair, chunk).start()

        relay(1, line, base + across, pair, chunk).start()
        relay(2, line, base + beside, pair, chunk).start()
        if spot:
            second(*order[spot - 1])
    second(*order[-1])

    for pair, chunk in order:
        relay(2, beside, base + beside, pair, chunk).wait_recv()
        relay(3, across_beside, base + beside, pair, chunk).wait_recv()

        @pl.when(inner)
        def _():
            relay(0, line, outward * 4 + line, pair, chunk).wait_send()
            burst(pair, chunk).wait_send()

        relay(1, line, base + across, pair, chunk).wait_send()
        relay(2, line, base + beside, pair, chunk).wait_send()
        relay(3, across, base + beside, pair, chunk).wait_send()

    def finish(step, carry):
        tile = target_of(step)
        tag(tile, tile).wait_recv()
        tag(tile, me).wait_send()

        @pl.when(tile // 4 != far)
        def _():
            parcel(tile, 1 - mine, tile, 1 - mine).wait_recv()
            parcel(tile, mine, tile, mine).wait_recv()

        @pl.when(takes(tile))
        def _():
            parcel(tile, 1 - mine, me, mine).wait_send()
            parcel(tile, mine, me, mine).wait_send()

        return carry

    lax.fori_loop(1, tile_count, finish, 0)
    parcel(me, 1 - mine, me, 1 - mine).wait_recv()
    parcel(me, 1 - mine, me, mine).wait_send()
    own.wait()
    own_tag.wait()


def combine_kernel(allowance, where, labels, arrived, relayed, spread, gather, looked, total, count, prods):
    far = where[0]
    mine = where[1]
    total[...] = jnp.zeros_like(total)
    for slot in range(SLOTS):
        count[slot] = 0

    def add(source, load):
        for slot in range(allowance):
            label = labels[source, 0, slot]

            @pl.when(label > 0)
            def _():
                count[label - 1] = count[label - 1] + 1
                for part in range(2):
                    total[part, label - 1] += load(part, slot).astype(jnp.float32)

    def one_source(source, carry):
        @pl.when(source // 4 != far)
        def _():
            add(source, lambda part, slot: arrived[part, source, pl.ds(slot * SHARD_HEIGHT, SHARD_HEIGHT)])

        @pl.when(source // 4 == far)
        def _():
            def load(part, slot):
                top = labels[source, 0, 2 * allowance + slot]
                return relayed[lax.rem(source, 4), part, pl.ds(top, SHARD_HEIGHT)]

            add(source, load)

        return carry

    lax.fori_loop(0, arrived.shape[1], one_source, 0)

    def one(level, carry):
        for side in range(2):
            slot = level * 2 + side
            divisor = jnp.maximum(count[slot], 1).astype(jnp.float32)
            first = (total[1, slot] / divisor).astype(jnp.bfloat16).astype(jnp.float32)
            second = (total[0, slot] / divisor).astype(jnp.bfloat16).astype(jnp.float32)
            same = first * second
            cross = first * jnp.concatenate([second[:, 2:], second[:, :2]], axis=1)
            for kind, value in ((0, same), (1, cross)):
                boxes = [jnp.sum(value[box * LOOK_ROWS : (box + 1) * LOOK_ROWS], axis=0) for box in range(4)]
                for two in range(2):
                    at = pl.ds(pl.multiple_of((level * 2 + two) * 8, 8), 8)
                    prods[side, kind, at, :] = jnp.concatenate(boxes[2 * two : 2 * two + 2], axis=0)
        return carry

    lax.fori_loop(0, PATCH_SHARD_LEVEL, one, 0)
    sub = lax.rem(lax.broadcasted_iota(jnp.int32, (256, 128), 0), 4)
    lane = lax.broadcasted_iota(jnp.int32, (256, 128), 1)
    column = lax.rem(lane, 64)
    sign = jnp.where(jnp.logical_and(lane >= 64, sub < 2), -1.0, 1.0)
    pooled = jnp.zeros((256, 128), jnp.float32)
    for side in range(2):
        wide = jnp.dot(prods[side, 0], spread[0], precision=EXACT, preferred_element_type=jnp.float32)
        wide += jnp.dot(prods[side, 1], spread[1], precision=EXACT, preferred_element_type=jnp.float32)
        pooled += jnp.where(column // 8 == side * 4 + mine * 2 + lax.rem(sub, 2), wide * sign, 0.0)
    looked[...] = jnp.dot(gather[...], pooled, precision=EXACT, preferred_element_type=jnp.float32)


def filter_kernel(looked, left, right, right_back, out, other, send_sem, recv_sem):
    mine = lax.axis_index("pair")
    barrier = pltpu.get_barrier_semaphore()
    pl.semaphore_signal(barrier, inc=1, device_id={"pair": 1 - mine}, device_id_type=MESH)
    pl.semaphore_wait(barrier, 1)
    copy = pltpu.make_async_remote_copy(
        src_ref=looked, dst_ref=other, send_sem=send_sem, recv_sem=recv_sem,
        device_id={"pair": 1 - mine}, device_id_type=MESH,
    )
    copy.start()

    def dot(a, b):
        return jnp.dot(a, b, precision=EXACT, preferred_element_type=jnp.float32)

    length = left.shape[1]
    lane = lax.broadcasted_iota(jnp.int32, (length, 2 * length), 1)
    turn = jnp.where(lane < length, 1.0, -1.0)
    flip = jnp.where(lane < length, 1.0, 1.0 - 2.0 * mine.astype(jnp.float32))
    copy.wait()
    field = (looked[...] + other[...]) * flip
    both = dot(left[...], field)
    spectrum = both[:length] + turn * pltpu.roll(both[length:], length, 1)
    spectrum = dot(spectrum, right[...])
    power = spectrum * spectrum
    power = power + pltpu.roll(power, length, 1)
    weight = jnp.sqrt(jnp.sqrt(power + 1e-06))
    mean = jnp.sum(weight) * (1.0 / (2 * length * length))
    spectrum = spectrum * (weight / mean)
    both = dot(left[...], spectrum)
    back = both[:length] - turn * pltpu.roll(both[length:], length, 1)
    back = dot(back, right_back[...]) * (1.0 / (length * length))
    out[0] = back[:, :length]
    out[1] = back[:, length:]


def constants():
    lane = np.arange(128)
    column = np.arange(64)
    pick = (lane[:, None] // LOOK_COLS == column[None, :] % 8).astype(np.float32)
    nil = np.zeros_like(pick)
    spread = np.stack([np.concatenate([pick, nil], 1), np.concatenate([nil, pick], 1)])
    gather = (column[:, None] == np.arange(256)[None, :] // 4).astype(np.float32)
    gather = gather / (LOOK_ROWS * LOOK_COLS)
    angle = (column[:, None] * column[None, :] % 64) * (2.0 * math.pi / 64)
    cosine, sine = np.cos(angle), np.sin(angle)
    left = np.concatenate([cosine, sine], 0)
    right = np.block([[cosine, -sine], [sine, cosine]])
    right_back = np.block([[cosine, sine], [-sine, cosine]])
    return (spread, gather), tuple(x.astype(np.float32) for x in (left, right, right_back))


def local_pair(coregistered_sweeps, shard_opening_height, shard_goal_patch, shard_patch_place):
    tile_count = lax.axis_size("ground")
    piece_count = shard_opening_height.shape[0]
    allowance = max(2, (2 * piece_count + tile_count - 1) // tile_count)
    pool, transforms = constants()
    smem = pl.BlockSpec(memory_space=pltpu.SMEM)
    vmem = pl.BlockSpec(memory_space=pltpu.VMEM)
    anyplace = pl.BlockSpec(memory_space=pl.ANY)
    starts, labels = pl.pallas_call(
        functools.partial(table_kernel, allowance),
        out_shape=(
            jax.ShapeDtypeStruct((tile_count, allowance), jnp.int32),
            jax.ShapeDtypeStruct((tile_count, 1, 128), jnp.int32),
        ),
        in_specs=[smem] * 3,
        out_specs=(smem, smem),
    )(shard_opening_height, shard_goal_patch[:, 0], shard_patch_place)
    height = coregistered_sweeps.shape[2]
    sweep = (
        coregistered_sweeps[0, 0]
        .reshape(height, 2, 2, 2, 128)
        .transpose(2, 0, 1, 3, 4)
        .reshape(2, height, 4, 128)
    )
    depth = allowance * SHARD_HEIGHT
    arrived, relayed, arrived_labels = pl.pallas_call(
        functools.partial(exchange_kernel, allowance),
        out_shape=(
            jax.ShapeDtypeStruct((2, tile_count, depth, 4, 128), jnp.bfloat16),
            jax.ShapeDtypeStruct((4, 2, height, 4, 128), jnp.bfloat16),
            jax.ShapeDtypeStruct((tile_count, 1, 128), jnp.int32),
        ),
        in_specs=[smem, vmem, vmem],
        out_specs=(anyplace, anyplace, vmem),
        scratch_shapes=[
            pltpu.VMEM((tile_count, 2, depth, 4, 128), jnp.bfloat16),
            pltpu.SemaphoreType.DMA((tile_count, 2)),
            pltpu.SemaphoreType.DMA((2, tile_count)),
            pltpu.SemaphoreType.DMA((tile_count,)),
            pltpu.SemaphoreType.DMA((tile_count,)),
            pltpu.SemaphoreType.DMA((2,)),
            pltpu.SemaphoreType.DMA((2, CHUNKS)),
            pltpu.SemaphoreType.DMA((4, 2, CHUNKS)),
            pltpu.SemaphoreType.DMA((4, 2, CHUNKS)),
        ],
        compiler_params=pltpu.CompilerParams(
            collective_id=0, has_side_effects=True, vmem_limit_bytes=16 * 1024 * 1024
        ),
    )(starts, labels, sweep)
    level = lax.axis_index("ground") // 4
    where = jnp.stack([2 - level // 2, lax.axis_index("pair")]).astype(jnp.int32)
    looked = pl.pallas_call(
        functools.partial(combine_kernel, allowance),
        out_shape=jax.ShapeDtypeStruct((64, 128), jnp.float32),
        in_specs=[smem, smem, vmem, vmem, vmem, vmem],
        out_specs=vmem,
        scratch_shapes=[
            pltpu.VMEM((2, SLOTS, SHARD_HEIGHT, 4, 128), jnp.float32),
            pltpu.SMEM((SLOTS,), jnp.int32),
            pltpu.VMEM((2, 2, 256, 128), jnp.float32),
        ],
        compiler_params=pltpu.CompilerParams(vmem_limit_bytes=24 * 1024 * 1024),
    )(where, arrived_labels, arrived, relayed, *pool)
    filtered = pl.pallas_call(
        filter_kernel,
        out_shape=jax.ShapeDtypeStruct((2, 64, 64), jnp.float32),
        in_specs=[vmem] * 4,
        out_specs=vmem,
        scratch_shapes=[
            pltpu.VMEM((64, 128), jnp.float32),
            pltpu.SemaphoreType.DMA,
            pltpu.SemaphoreType.DMA,
        ],
        compiler_params=pltpu.CompilerParams(collective_id=1, has_side_effects=True),
    )(looked, *transforms)
    return filtered[None, None, None]


def solution(mesh):
    if mesh.shape["pair"] != 2 or mesh.shape["ground"] != 16:
        return general(mesh)
    placed = (P("pair", "ground", None, None, None), P("ground"), P("ground", None), P("ground"))
    return jax.shard_map(
        local_pair,
        mesh=mesh,
        in_specs=placed,
        out_specs=P("pair", None, "ground", None, None, None),
        check_vma=False,
    )
```

```python
import functools
import math

import jax
import jax.numpy as jnp
import numpy as np
from jax import lax
from jax.experimental import pallas as pl
from jax.experimental.pallas import tpu as pltpu
from jax.sharding import PartitionSpec as P

LOOK_ROWS = 4
LOOK_COLS = 16
SHARD_HEIGHT = 16
TILE_ROWS = 256
TILE_COLS = 1024
SWEEP_WIDTH = 512
PATCH_SHARD_LEVEL = 16
SLOTS = 32


def multilook(reference_tiles, secondary_tiles):
    first = reference_tiles.astype(jnp.float32)
    second = secondary_tiles.astype(jnp.float32)
    real_part = first[..., 0, :] * second[..., 0, :] + first[..., 1, :] * second[..., 1, :]
    imag_part = first[..., 1, :] * second[..., 0, :] - first[..., 0, :] * second[..., 1, :]
    joined = jnp.stack([real_part, imag_part], axis=-3)
    leading = joined.shape[:-2]
    row_count = joined.shape[-2]
    col_count = joined.shape[-1]
    boxes = joined.reshape(
        leading + (row_count // LOOK_ROWS, LOOK_ROWS, col_count // LOOK_COLS, LOOK_COLS)
    )
    return jnp.mean(boxes, axis=(-3, -1))


def on_left(matrix, field):
    return jnp.einsum("ij,...jk->...ik", matrix, field, precision=lax.Precision.HIGHEST)


def on_right(field, matrix):
    return jnp.einsum("...ij,jk->...ik", field, matrix, precision=lax.Precision.HIGHEST)


def goldstein(looked):
    length = looked.shape[-1]
    positions = jnp.arange(length, dtype=jnp.int32)
    phase = positions[:, None] * positions[None, :] % length
    angle = phase.astype(jnp.float32) * (2.0 * math.pi / length)
    cosine = jnp.cos(angle)
    sine = jnp.sin(angle)
    real_in = looked[..., 0, :, :]
    imag_in = looked[..., 1, :, :]
    half_real = on_left(cosine, real_in) + on_left(sine, imag_in)
    half_imag = on_left(cosine, imag_in) - on_left(sine, real_in)
    spec_real = on_right(half_real, cosine) + on_right(half_imag, sine)
    spec_imag = on_right(half_imag, cosine) - on_right(half_real, sine)
    weight = (spec_real * spec_real + spec_imag * spec_imag + 1e-06) ** 0.25
    weight = weight / jnp.mean(weight, axis=(-2, -1), keepdims=True)
    spec_real = spec_real * weight
    spec_imag = spec_imag * weight
    back_real = on_left(cosine, spec_real) - on_left(sine, spec_imag)
    back_imag = on_left(cosine, spec_imag) + on_left(sine, spec_real)
    out_real = on_right(back_real, cosine) - on_right(back_imag, sine)
    out_imag = on_right(back_imag, cosine) + on_right(back_real, sine)
    scale = 1.0 / (length * length)
    return jnp.stack([out_real * scale, out_imag * scale], axis=-3)


def partners_of(index, pair_width):
    order = jnp.arange(pair_width, dtype=jnp.int32)
    return order + (order >= index).astype(jnp.int32)


def local(coregistered_sweeps, shard_opening_height, shard_goal_patch, shard_patch_place):
    earth_patch_total_size = lax.axis_size("ground")
    pair_count = lax.axis_size("pair")
    piece_count = shard_opening_height.shape[0]
    place_allowance = max(
        2, (2 * piece_count + earth_patch_total_size - 1) // earth_patch_total_size
    )
    sweep_resident = coregistered_sweeps[0, 0]
    target = shard_goal_patch[:, 0]
    hits = (target[:, None] == jnp.arange(earth_patch_total_size, dtype=jnp.int32)[None, :]).astype(
        jnp.int32
    )
    earlier = jnp.cumsum(hits, axis=0) - hits
    rank = jnp.sum(earlier * hits, axis=1)
    position = target * place_allowance + rank
    matches = (
        position[None, :]
        == jnp.arange(earth_patch_total_size * place_allowance, dtype=jnp.int32)[:, None]
    ).astype(jnp.int32)
    tiles_filled = jnp.sum(matches, axis=1) > 0
    chosen = jnp.sum(matches * jnp.arange(piece_count, dtype=jnp.int32)[None, :], axis=1)
    sweep_height_offset = (
        shard_opening_height[chosen][:, None] + jnp.arange(SHARD_HEIGHT, dtype=jnp.int32)[None, :]
    )
    pieces_to_send = jnp.where(
        tiles_filled[:, None, None, None],
        sweep_resident[sweep_height_offset],
        jnp.zeros((), jnp.bfloat16),
    )
    labels = jnp.where(tiles_filled, shard_patch_place[chosen] + 1, 0).astype(jnp.bfloat16)
    received_pieces, arrived_labels = (
        lax.all_to_all(
            pieces_to_send.reshape(
                earth_patch_total_size, place_allowance, SHARD_HEIGHT, 2, SWEEP_WIDTH
            ),
            "ground",
            split_axis=0,
            concat_axis=0,
            tiled=True,
        ),
        lax.all_to_all(
            labels.reshape(earth_patch_total_size, place_allowance),
            "ground",
            split_axis=0,
            concat_axis=0,
            tiled=True,
        ),
    )
    pieces_flattened = received_pieces.reshape(
        earth_patch_total_size * place_allowance, SHARD_HEIGHT * 2 * SWEEP_WIDTH
    )
    slot_labels = (jnp.arange(SLOTS, dtype=jnp.int32) + 1).astype(jnp.bfloat16)
    selector = arrived_labels.reshape(-1)[None, :] == slot_labels[:, None]
    totals = jnp.dot(
        selector.astype(jnp.bfloat16), pieces_flattened, preferred_element_type=jnp.float32
    )
    counts = jnp.sum(selector.astype(jnp.float32), axis=1)
    smoothed_pixel_mean = (totals / jnp.maximum(counts, 1.0)[:, None]).astype(jnp.bfloat16)
    ground_tile = (
        smoothed_pixel_mean.reshape(PATCH_SHARD_LEVEL, 2, SHARD_HEIGHT, 2, SWEEP_WIDTH)
        .transpose(0, 2, 3, 1, 4)
        .reshape(TILE_ROWS, 2, TILE_COLS)
    )
    pair_width = pair_count - 1
    own_refs = partners_of(lax.axis_index("pair"), pair_width)
    piece = lax.all_gather(ground_tile[None], "pair", axis=0, tiled=True)
    looked_piece = multilook(piece, ground_tile[None])
    indices = jnp.arange(piece.shape[0], dtype=jnp.int32)
    selection = (own_refs[:, None] == indices[None, :]).astype(jnp.float32)
    looked = jnp.einsum("kn,nabc->kabc", selection, looked_piece, precision=lax.Precision.HIGHEST)
    return goldstein(looked)[None, :, None]


def general(mesh):
    placed = (P("pair", "ground", None, None, None), P("ground"), P("ground", None), P("ground"))
    return jax.shard_map(
        local,
        mesh=mesh,
        in_specs=placed,
        out_specs=P("pair", None, "ground", None, None, None),
        check_vma=False,
    )


CHUNKS = 4
MESH = pl.DeviceIdType.MESH
EXACT = lax.Precision.HIGHEST


def table_kernel(allowance, opening, goal, place, starts, labels):
    tile_count = starts.shape[0]

    def clear(tile, carry):
        for slot in range(allowance):
            starts[tile, slot] = 0
            labels[tile, 0, slot] = 0
            labels[tile, 0, 2 * allowance + slot] = 0
        labels[tile, 0, allowance] = 0
        return carry

    lax.fori_loop(0, tile_count, clear, 0)

    def enter(piece, carry):
        tile = goal[piece]
        rank = labels[tile, 0, allowance]
        starts[tile, rank] = opening[piece]
        labels[tile, 0, rank] = place[piece] + 1
        labels[tile, 0, 2 * allowance + rank] = opening[piece]
        labels[tile, 0, allowance] = rank + 1
        return carry

    lax.fori_loop(0, opening.shape[0], enter, 0)


def exchange_kernel(
    allowance, starts, labels, sweep, arrived, relayed, arrived_labels,
    outgoing, send_sem, recv_sem, label_send, label_recv, own_sem,
    burst_send, relay_send, relay_recv,
):
    me = lax.axis_index("ground")
    mine = lax.axis_index("pair")
    tile_count = 16
    level = me // 4
    line = lax.rem(me, 4)
    across = lax.rem(line + 2, 4)
    beside = line + 1 - 2 * lax.rem(line, 2)
    across_beside = lax.rem(beside + 2, 4)
    inner = jnp.logical_or(level == 1, level == 2)
    right = level // 2
    outward = 3 * right
    far = 2 - right
    barrier = pltpu.get_barrier_semaphore()

    def greet(step, carry):
        pl.semaphore_signal(
            barrier, inc=1,
            device_id={"ground": lax.rem(me + step // 2, tile_count), "pair": lax.rem(mine + step, 2)},
            device_id_type=MESH,
        )
        return carry

    lax.fori_loop(1, 2 * tile_count, greet, 0)

    def extract(tile):
        def one(slot, carry):
            top = starts[tile, slot]
            for part in range(2):
                outgoing[tile, part, pl.ds(slot * SHARD_HEIGHT, SHARD_HEIGHT)] = sweep[
                    part, pl.ds(top, SHARD_HEIGHT)
                ]
            return carry

        lax.fori_loop(0, allowance, one, 0)

    def parcel(tile, other, source, source_pair):
        return pltpu.make_async_remote_copy(
            src_ref=outgoing.at[tile, other],
            dst_ref=arrived.at[source_pair, source],
            send_sem=send_sem.at[tile, other],
            recv_sem=recv_sem.at[source_pair, source],
            device_id={"ground": tile, "pair": other},
            device_id_type=MESH,
        )

    def tag(tile, source):
        return pltpu.make_async_remote_copy(
            src_ref=labels.at[tile],
            dst_ref=arrived_labels.at[source],
            send_sem=label_send.at[tile],
            recv_sem=label_recv.at[source],
            device_id={"ground": tile, "pair": mine},
            device_id_type=MESH,
        )

    span = sweep.shape[1] // CHUNKS

    def burst(part, chunk):
        rows = pl.ds(chunk * span, span)
        return pltpu.make_async_remote_copy(
            src_ref=sweep.at[part, rows],
            dst_ref=relayed.at[line, mine, rows],
            send_sem=burst_send.at[part, chunk],
            recv_sem=relay_recv.at[line, mine, chunk],
            device_id={"ground": far * 4 + line, "pair": part},
            device_id_type=MESH,
        )

    def relay(kind, which, target, pair, chunk):
        rows = pl.ds(chunk * span, span)
        return pltpu.make_async_remote_copy(
            src_ref=relayed.at[which, pair, rows],
            dst_ref=relayed.at[which, pair, rows],
            send_sem=relay_send.at[kind, pair, chunk],
            recv_sem=relay_recv.at[which, pair, chunk],
            device_id={"ground": target, "pair": mine},
            device_id_type=MESH,
        )

    def target_of(step):
        return lax.rem(me + step, tile_count)

    def takes(tile):
        return jnp.logical_or(jnp.logical_not(inner), tile // 8 == right)

    def send(tile):
        tag(tile, me).start()

        @pl.when(takes(tile))
        def _():
            extract(tile)
            parcel(tile, 1 - mine, me, mine).start()
            parcel(tile, mine, me, mine).start()

    pl.semaphore_wait(barrier, 2 * tile_count - 1)

    @pl.when(inner)
    def _():
        for chunk in range(CHUNKS):
            for part in range(2):
                burst(part, chunk).start()

    mirror = level + right * (3 - 2 * level)

    def near(step, carry):
        distance = 1 - lax.rem(step, 2)
        place = distance + mirror - 2 * distance * mirror
        tile = (place + right * (3 - 2 * place)) * 4 + lax.rem(line + 1 + step // 2, 4)

        @pl.when(tile != me)
        def _():
            send(tile)

        return carry

    def away(step, carry):
        place = 3 - lax.rem(step, 2)
        send((place + right * (3 - 2 * place)) * 4 + lax.rem(line + 1 + step // 2, 4))
        return carry

    lax.fori_loop(0, 8, near, 0)
    lax.fori_loop(0, 8, away, 0)
    extract(me)
    parcel(me, 1 - mine, me, mine).start()
    own = pltpu.make_async_copy(outgoing.at[me, mine], arrived.at[mine, me], own_sem.at[0])
    own.start()
    own_tag = pltpu.make_async_copy(labels.at[me], arrived_labels.at[me], own_sem.at[1])
    own_tag.start()

    base = level * 4
    order = [(pair, chunk) for chunk in range(CHUNKS) for pair in range(2)]

    def second(pair, chunk):
        relay(1, across, base + across, pair, chunk).wait_recv()
        relay(3, across, base + beside, pair, chunk).start()

    for spot, (pair, chunk) in enumerate(order):
        relay(0, line, base + across, pair, chunk).wait_recv()

        @pl.when(inner)
        def _():
            relay(0, line, outward * 4 + line, pair, chunk).start()

        relay(1, line, base + across, pair, chunk).start()
        relay(2, line, base + beside, pair, chunk).start()
        if spot:
            second(*order[spot - 1])
    second(*order[-1])

    for pair, chunk in order:
        relay(2, beside, base + beside, pair, chunk).wait_recv()
        relay(3, across_beside, base + beside, pair, chunk).wait_recv()

        @pl.when(inner)
        def _():
            relay(0, line, outward * 4 + line, pair, chunk).wait_send()
            burst(pair, chunk).wait_send()

        relay(1, line, base + across, pair, chunk).wait_send()
        relay(2, line, base + beside, pair, chunk).wait_send()
        relay(3, across, base + beside, pair, chunk).wait_send()

    def finish(step, carry):
        tile = target_of(step)
        tag(tile, tile).wait_recv()
        tag(tile, me).wait_send()

        @pl.when(tile // 4 != far)
        def _():
            parcel(tile, 1 - mine, tile, 1 - mine).wait_recv()
            parcel(tile, mine, tile, mine).wait_recv()

        @pl.when(takes(tile))
        def _():
            parcel(tile, 1 - mine, me, mine).wait_send()
            parcel(tile, mine, me, mine).wait_send()

        return carry

    lax.fori_loop(1, tile_count, finish, 0)
    parcel(me, 1 - mine, me, 1 - mine).wait_recv()
    parcel(me, 1 - mine, me, mine).wait_send()
    own.wait()
    own_tag.wait()


def combine_kernel(allowance, where, labels, arrived, relayed, spread, gather, looked, total, count, prods):
    far = where[0]
    mine = where[1]
    total[...] = jnp.zeros_like(total)
    for slot in range(SLOTS):
        count[slot] = 0

    def add(source, load):
        for slot in range(allowance):
            label = labels[source, 0, slot]

            @pl.when(label > 0)
            def _():
                count[label - 1] = count[label - 1] + 1
                for part in range(2):
                    total[part, label - 1] += load(part, slot).astype(jnp.float32)

    def one_source(source, carry):
        @pl.when(source // 4 != far)
        def _():
            add(source, lambda part, slot: arrived[part, source, pl.ds(slot * SHARD_HEIGHT, SHARD_HEIGHT)])

        @pl.when(source // 4 == far)
        def _():
            def load(part, slot):
                top = labels[source, 0, 2 * allowance + slot]
                return relayed[lax.rem(source, 4), part, pl.ds(top, SHARD_HEIGHT)]

            add(source, load)

        return carry

    lax.fori_loop(0, arrived.shape[1], one_source, 0)

    def one(level, carry):
        for side in range(2):
            slot = level * 2 + side
            divisor = jnp.maximum(count[slot], 1).astype(jnp.float32)
            first = (total[1, slot] / divisor).astype(jnp.bfloat16).astype(jnp.float32)
            second = (total[0, slot] / divisor).astype(jnp.bfloat16).astype(jnp.float32)
            same = first * second
            cross = first * jnp.concatenate([second[:, 2:], second[:, :2]], axis=1)
            for kind, value in ((0, same), (1, cross)):
                boxes = [jnp.sum(value[box * LOOK_ROWS : (box + 1) * LOOK_ROWS], axis=0) for box in range(4)]
                for two in range(2):
                    at = pl.ds(pl.multiple_of((level * 2 + two) * 8, 8), 8)
                    prods[side, kind, at, :] = jnp.concatenate(boxes[2 * two : 2 * two + 2], axis=0)
        return carry

    lax.fori_loop(0, PATCH_SHARD_LEVEL, one, 0)
    sub = lax.rem(lax.broadcasted_iota(jnp.int32, (256, 128), 0), 4)
    lane = lax.broadcasted_iota(jnp.int32, (256, 128), 1)
    column = lax.rem(lane, 64)
    sign = jnp.where(jnp.logical_and(lane >= 64, sub < 2), -1.0, 1.0)
    pooled = jnp.zeros((256, 128), jnp.float32)
    for side in range(2):
        wide = jnp.dot(prods[side, 0], spread[0], precision=EXACT, preferred_element_type=jnp.float32)
        wide += jnp.dot(prods[side, 1], spread[1], precision=EXACT, preferred_element_type=jnp.float32)
        pooled += jnp.where(column // 8 == side * 4 + mine * 2 + lax.rem(sub, 2), wide * sign, 0.0)
    looked[...] = jnp.dot(gather[...], pooled, precision=EXACT, preferred_element_type=jnp.float32)


def filter_kernel(looked, left, right, right_back, out, other, send_sem, recv_sem):
    mine = lax.axis_index("pair")
    barrier = pltpu.get_barrier_semaphore()
    pl.semaphore_signal(barrier, inc=1, device_id={"pair": 1 - mine}, device_id_type=MESH)
    pl.semaphore_wait(barrier, 1)
    copy = pltpu.make_async_remote_copy(
        src_ref=looked, dst_ref=other, send_sem=send_sem, recv_sem=recv_sem,
        device_id={"pair": 1 - mine}, device_id_type=MESH,
    )
    copy.start()

    def dot(a, b):
        return jnp.dot(a, b, precision=EXACT, preferred_element_type=jnp.float32)

    length = left.shape[1]
    lane = lax.broadcasted_iota(jnp.int32, (length, 2 * length), 1)
    turn = jnp.where(lane < length, 1.0, -1.0)
    flip = jnp.where(lane < length, 1.0, 1.0 - 2.0 * mine.astype(jnp.float32))
    copy.wait()
    field = (looked[...] + other[...]) * flip
    both = dot(left[...], field)
    spectrum = both[:length] + turn * pltpu.roll(both[length:], length, 1)
    spectrum = dot(spectrum, right[...])
    power = spectrum * spectrum
    power = power + pltpu.roll(power, length, 1)
    weight = jnp.sqrt(jnp.sqrt(power + 1e-06))
    mean = jnp.sum(weight) * (1.0 / (2 * length * length))
    spectrum = spectrum * (weight / mean)
    both = dot(left[...], spectrum)
    back = both[:length] - turn * pltpu.roll(both[length:], length, 1)
    back = dot(back, right_back[...]) * (1.0 / (length * length))
    out[0] = back[:, :length]
    out[1] = back[:, length:]


def constants():
    lane = np.arange(128)
    column = np.arange(64)
    pick = (lane[:, None] // LOOK_COLS == column[None, :] % 8).astype(np.float32)
    nil = np.zeros_like(pick)
    spread = np.stack([np.concatenate([pick, nil], 1), np.concatenate([nil, pick], 1)])
    gather = (column[:, None] == np.arange(256)[None, :] // 4).astype(np.float32)
    gather = gather / (LOOK_ROWS * LOOK_COLS)
    angle = (column[:, None] * column[None, :] % 64) * (2.0 * math.pi / 64)
    cosine, sine = np.cos(angle), np.sin(angle)
    left = np.concatenate([cosine, sine], 0)
    right = np.block([[cosine, -sine], [sine, cosine]])
    right_back = np.block([[cosine, sine], [-sine, cosine]])
    return (spread, gather), tuple(x.astype(np.float32) for x in (left, right, right_back))


def local_pair(coregistered_sweeps, shard_opening_height, shard_goal_patch, shard_patch_place):
    tile_count = lax.axis_size("ground")
    piece_count = shard_opening_height.shape[0]
    allowance = max(2, (2 * piece_count + tile_count - 1) // tile_count)
    pool, transforms = constants()
    smem = pl.BlockSpec(memory_space=pltpu.SMEM)
    vmem = pl.BlockSpec(memory_space=pltpu.VMEM)
    anyplace = pl.BlockSpec(memory_space=pl.ANY)
    starts, labels = pl.pallas_call(
        functools.partial(table_kernel, allowance),
        out_shape=(
            jax.ShapeDtypeStruct((tile_count, allowance), jnp.int32),
            jax.ShapeDtypeStruct((tile_count, 1, 128), jnp.int32),
        ),
        in_specs=[smem] * 3,
        out_specs=(smem, smem),
    )(shard_opening_height, shard_goal_patch[:, 0], shard_patch_place)
    height = coregistered_sweeps.shape[2]
    sweep = (
        coregistered_sweeps[0, 0]
        .reshape(height, 2, 2, 2, 128)
        .transpose(2, 0, 1, 3, 4)
        .reshape(2, height, 4, 128)
    )
    depth = allowance * SHARD_HEIGHT
    arrived, relayed, arrived_labels = pl.pallas_call(
        functools.partial(exchange_kernel, allowance),
        out_shape=(
            jax.ShapeDtypeStruct((2, tile_count, depth, 4, 128), jnp.bfloat16),
            jax.ShapeDtypeStruct((4, 2, height, 4, 128), jnp.bfloat16),
            jax.ShapeDtypeStruct((tile_count, 1, 128), jnp.int32),
        ),
        in_specs=[smem, vmem, vmem],
        out_specs=(anyplace, anyplace, vmem),
        scratch_shapes=[
            pltpu.VMEM((tile_count, 2, depth, 4, 128), jnp.bfloat16),
            pltpu.SemaphoreType.DMA((tile_count, 2)),
            pltpu.SemaphoreType.DMA((2, tile_count)),
            pltpu.SemaphoreType.DMA((tile_count,)),
            pltpu.SemaphoreType.DMA((tile_count,)),
            pltpu.SemaphoreType.DMA((2,)),
            pltpu.SemaphoreType.DMA((2, CHUNKS)),
            pltpu.SemaphoreType.DMA((4, 2, CHUNKS)),
            pltpu.SemaphoreType.DMA((4, 2, CHUNKS)),
        ],
        compiler_params=pltpu.CompilerParams(
            collective_id=0, has_side_effects=True, vmem_limit_bytes=16 * 1024 * 1024
        ),
    )(starts, labels, sweep)
    level = lax.axis_index("ground") // 4
    where = jnp.stack([2 - level // 2, lax.axis_index("pair")]).astype(jnp.int32)
    looked = pl.pallas_call(
        functools.partial(combine_kernel, allowance),
        out_shape=jax.ShapeDtypeStruct((64, 128), jnp.float32),
        in_specs=[smem, smem, vmem, vmem, vmem, vmem],
        out_specs=vmem,
        scratch_shapes=[
            pltpu.VMEM((2, SLOTS, SHARD_HEIGHT, 4, 128), jnp.float32),
            pltpu.SMEM((SLOTS,), jnp.int32),
            pltpu.VMEM((2, 2, 256, 128), jnp.float32),
        ],
        compiler_params=pltpu.CompilerParams(vmem_limit_bytes=24 * 1024 * 1024),
    )(where, arrived_labels, arrived, relayed, *pool)
    filtered = pl.pallas_call(
        filter_kernel,
        out_shape=jax.ShapeDtypeStruct((2, 64, 64), jnp.float32),
        in_specs=[vmem] * 4,
        out_specs=vmem,
        scratch_shapes=[
            pltpu.VMEM((64, 128), jnp.float32),
            pltpu.SemaphoreType.DMA,
            pltpu.SemaphoreType.DMA,
        ],
        compiler_params=pltpu.CompilerParams(collective_id=1, has_side_effects=True),
    )(looked, *transforms)
    return filtered[None, None, None]


def solution(mesh):
    if mesh.shape["pair"] != 2 or mesh.shape["ground"] != 16:
        return general(mesh)
    placed = (P("pair", "ground", None, None, None), P("ground"), P("ground", None), P("ground"))
    return jax.shard_map(
        local_pair,
        mesh=mesh,
        in_specs=placed,
        out_specs=P("pair", None, "ground", None, None, None),
        check_vma=False,
    )
```

```python
import functools
import math

import jax
import jax.numpy as jnp
import numpy as np
from jax import lax
from jax.experimental import pallas as pl
from jax.experimental.pallas import tpu as pltpu
from jax.sharding import PartitionSpec as P

LOOK_ROWS = 4
LOOK_COLS = 16
SHARD_HEIGHT = 16
TILE_ROWS = 256
TILE_COLS = 1024
SWEEP_WIDTH = 512
PATCH_SHARD_LEVEL = 16
SLOTS = 32


def multilook(reference_tiles, secondary_tiles):
    first = reference_tiles.astype(jnp.float32)
    second = secondary_tiles.astype(jnp.float32)
    real_part = first[..., 0, :] * second[..., 0, :] + first[..., 1, :] * second[..., 1, :]
    imag_part = first[..., 1, :] * second[..., 0, :] - first[..., 0, :] * second[..., 1, :]
    joined = jnp.stack([real_part, imag_part], axis=-3)
    leading = joined.shape[:-2]
    row_count = joined.shape[-2]
    col_count = joined.shape[-1]
    boxes = joined.reshape(
        leading + (row_count // LOOK_ROWS, LOOK_ROWS, col_count // LOOK_COLS, LOOK_COLS)
    )
    return jnp.mean(boxes, axis=(-3, -1))


def on_left(matrix, field):
    return jnp.einsum("ij,...jk->...ik", matrix, field, precision=lax.Precision.HIGHEST)


def on_right(field, matrix):
    return jnp.einsum("...ij,jk->...ik", field, matrix, precision=lax.Precision.HIGHEST)


def goldstein(looked):
    length = looked.shape[-1]
    positions = jnp.arange(length, dtype=jnp.int32)
    phase = positions[:, None] * positions[None, :] % length
    angle = phase.astype(jnp.float32) * (2.0 * math.pi / length)
    cosine = jnp.cos(angle)
    sine = jnp.sin(angle)
    real_in = looked[..., 0, :, :]
    imag_in = looked[..., 1, :, :]
    half_real = on_left(cosine, real_in) + on_left(sine, imag_in)
    half_imag = on_left(cosine, imag_in) - on_left(sine, real_in)
    spec_real = on_right(half_real, cosine) + on_right(half_imag, sine)
    spec_imag = on_right(half_imag, cosine) - on_right(half_real, sine)
    weight = (spec_real * spec_real + spec_imag * spec_imag + 1e-06) ** 0.25
    weight = weight / jnp.mean(weight, axis=(-2, -1), keepdims=True)
    spec_real = spec_real * weight
    spec_imag = spec_imag * weight
    back_real = on_left(cosine, spec_real) - on_left(sine, spec_imag)
    back_imag = on_left(cosine, spec_imag) + on_left(sine, spec_real)
    out_real = on_right(back_real, cosine) - on_right(back_imag, sine)
    out_imag = on_right(back_imag, cosine) + on_right(back_real, sine)
    scale = 1.0 / (length * length)
    return jnp.stack([out_real * scale, out_imag * scale], axis=-3)


def partners_of(index, pair_width):
    order = jnp.arange(pair_width, dtype=jnp.int32)
    return order + (order >= index).astype(jnp.int32)


def local(coregistered_sweeps, shard_opening_height, shard_goal_patch, shard_patch_place):
    earth_patch_total_size = lax.axis_size("ground")
    pair_count = lax.axis_size("pair")
    piece_count = shard_opening_height.shape[0]
    place_allowance = max(
        2, (2 * piece_count + earth_patch_total_size - 1) // earth_patch_total_size
    )
    sweep_resident = coregistered_sweeps[0, 0]
    target = shard_goal_patch[:, 0]
    hits = (target[:, None] == jnp.arange(earth_patch_total_size, dtype=jnp.int32)[None, :]).astype(
        jnp.int32
    )
    earlier = jnp.cumsum(hits, axis=0) - hits
    rank = jnp.sum(earlier * hits, axis=1)
    position = target * place_allowance + rank
    matches = (
        position[None, :]
        == jnp.arange(earth_patch_total_size * place_allowance, dtype=jnp.int32)[:, None]
    ).astype(jnp.int32)
    tiles_filled = jnp.sum(matches, axis=1) > 0
    chosen = jnp.sum(matches * jnp.arange(piece_count, dtype=jnp.int32)[None, :], axis=1)
    sweep_height_offset = (
        shard_opening_height[chosen][:, None] + jnp.arange(SHARD_HEIGHT, dtype=jnp.int32)[None, :]
    )
    pieces_to_send = jnp.where(
        tiles_filled[:, None, None, None],
        sweep_resident[sweep_height_offset],
        jnp.zeros((), jnp.bfloat16),
    )
    labels = jnp.where(tiles_filled, shard_patch_place[chosen] + 1, 0).astype(jnp.bfloat16)
    received_pieces, arrived_labels = (
        lax.all_to_all(
            pieces_to_send.reshape(
                earth_patch_total_size, place_allowance, SHARD_HEIGHT, 2, SWEEP_WIDTH
            ),
            "ground",
            split_axis=0,
            concat_axis=0,
            tiled=True,
        ),
        lax.all_to_all(
            labels.reshape(earth_patch_total_size, place_allowance),
            "ground",
            split_axis=0,
            concat_axis=0,
            tiled=True,
        ),
    )
    pieces_flattened = received_pieces.reshape(
        earth_patch_total_size * place_allowance, SHARD_HEIGHT * 2 * SWEEP_WIDTH
    )
    slot_labels = (jnp.arange(SLOTS, dtype=jnp.int32) + 1).astype(jnp.bfloat16)
    selector = arrived_labels.reshape(-1)[None, :] == slot_labels[:, None]
    totals = jnp.dot(
        selector.astype(jnp.bfloat16), pieces_flattened, preferred_element_type=jnp.float32
    )
    counts = jnp.sum(selector.astype(jnp.float32), axis=1)
    smoothed_pixel_mean = (totals / jnp.maximum(counts, 1.0)[:, None]).astype(jnp.bfloat16)
    ground_tile = (
        smoothed_pixel_mean.reshape(PATCH_SHARD_LEVEL, 2, SHARD_HEIGHT, 2, SWEEP_WIDTH)
        .transpose(0, 2, 3, 1, 4)
        .reshape(TILE_ROWS, 2, TILE_COLS)
    )
    pair_width = pair_count - 1
    own_refs = partners_of(lax.axis_index("pair"), pair_width)
    piece = lax.all_gather(ground_tile[None], "pair", axis=0, tiled=True)
    looked_piece = multilook(piece, ground_tile[None])
    indices = jnp.arange(piece.shape[0], dtype=jnp.int32)
    selection = (own_refs[:, None] == indices[None, :]).astype(jnp.float32)
    looked = jnp.einsum("kn,nabc->kabc", selection, looked_piece, precision=lax.Precision.HIGHEST)
    return goldstein(looked)[None, :, None]


def general(mesh):
    placed = (P("pair", "ground", None, None, None), P("ground"), P("ground", None), P("ground"))
    return jax.shard_map(
        local,
        mesh=mesh,
        in_specs=placed,
        out_specs=P("pair", None, "ground", None, None, None),
        check_vma=False,
    )


MESH = pl.DeviceIdType.MESH
EXACT = lax.Precision.HIGHEST


def table_kernel(allowance, opening, goal, place, starts, labels):
    tile_count = starts.shape[0]

    def clear(tile, carry):
        for slot in range(allowance):
            starts[tile, slot] = 0
            labels[tile, 0, slot] = 0
            labels[tile, 0, 2 * allowance + slot] = 0
        labels[tile, 0, allowance] = 0
        return carry

    lax.fori_loop(0, tile_count, clear, 0)

    def enter(piece, carry):
        tile = goal[piece]
        rank = labels[tile, 0, allowance]
        starts[tile, rank] = opening[piece]
        labels[tile, 0, rank] = place[piece] + 1
        labels[tile, 0, 2 * allowance + rank] = opening[piece]
        labels[tile, 0, allowance] = rank + 1
        return carry

    lax.fori_loop(0, opening.shape[0], enter, 0)


def exchange_kernel(
    allowance, starts, labels, sweep, arrived, arrived_labels,
    outgoing, send_sem, recv_sem, label_send, label_recv, own_sem,
    first_half, second_half, proxied, far_table, far_starts, burst_send, burst_recv, table_sem, proxy_sem,
):
    me = lax.axis_index("ground")
    mine = lax.axis_index("pair")
    tile_count = 16
    level = me // 4
    line = lax.rem(me, 4)
    inner = jnp.logical_or(level == 1, level == 2)
    right = level // 2
    far = 2 - right
    barrier = pltpu.get_barrier_semaphore()

    def greet(step, carry):
        pl.semaphore_signal(
            barrier, inc=1,
            device_id={"ground": lax.rem(me + step // 2, tile_count), "pair": lax.rem(mine + step, 2)},
            device_id_type=MESH,
        )
        return carry

    lax.fori_loop(1, 2 * tile_count, greet, 0)

    def extract(tile):
        def one(slot, carry):
            top = starts[tile, slot]
            for part in range(2):
                outgoing[tile, part, pl.ds(slot * SHARD_HEIGHT, SHARD_HEIGHT)] = sweep[
                    part, pl.ds(top, SHARD_HEIGHT)
                ]
            return carry

        lax.fori_loop(0, allowance, one, 0)

    def parcel(tile, other, source, source_pair):
        return pltpu.make_async_remote_copy(
            src_ref=outgoing.at[tile, other],
            dst_ref=arrived.at[source_pair, source],
            send_sem=send_sem.at[tile, other],
            recv_sem=recv_sem.at[source_pair, source],
            device_id={"ground": tile, "pair": other},
            device_id_type=MESH,
        )

    def tag(tile, source):
        return pltpu.make_async_remote_copy(
            src_ref=labels.at[tile],
            dst_ref=arrived_labels.at[source],
            send_sem=label_send.at[tile],
            recv_sem=label_recv.at[source],
            device_id={"ground": tile, "pair": mine},
            device_id_type=MESH,
        )

    far_me = far * 4 + line

    halves = (first_half, second_half)

    def burst(part, pair):
        return pltpu.make_async_remote_copy(
            src_ref=sweep.at[part],
            dst_ref=halves[pair],
            send_sem=burst_send.at[part],
            recv_sem=burst_recv.at[pair],
            device_id={"ground": far_me, "pair": part},
            device_id_type=MESH,
        )

    def far_rows():
        return pltpu.make_async_remote_copy(
            src_ref=labels.at[pl.ds(8 * (1 - right), 8)],
            dst_ref=far_table,
            send_sem=table_sem.at[0],
            recv_sem=table_sem.at[1],
            device_id={"ground": far_me, "pair": mine},
            device_id_type=MESH,
        )

    def proxy(index, pair):
        return pltpu.make_async_remote_copy(
            src_ref=proxied.at[index, pair],
            dst_ref=arrived.at[pair, far_me],
            send_sem=proxy_sem.at[index, pair],
            recv_sem=recv_sem.at[pair, far_me],
            device_id={"ground": 8 * right + index, "pair": mine},
            device_id_type=MESH,
        )

    def proxy_own(pair):
        index = me - 8 * right
        return pltpu.make_async_copy(
            proxied.at[index, pair], arrived.at[pair, far_me], proxy_sem.at[index, pair]
        )

    def target_of(step):
        return lax.rem(me + step, tile_count)

    def takes(tile):
        return jnp.logical_or(jnp.logical_not(inner), tile // 8 == right)

    def send(tile):
        tag(tile, me).start()

        @pl.when(takes(tile))
        def _():
            extract(tile)
            parcel(tile, 1 - mine, me, mine).start()
            parcel(tile, mine, me, mine).start()

    pl.semaphore_wait(barrier, 2 * tile_count - 1)

    @pl.when(inner)
    def _():
        far_rows().start()
        for pair in range(2):

            @pl.when(mine == pair)
            def _():
                for part in range(2):
                    burst(part, pair).start()

    mirror = level + right * (3 - 2 * level)

    def near(step, carry):
        distance = 1 - lax.rem(step, 2)
        place = distance + mirror - 2 * distance * mirror
        tile = (place + right * (3 - 2 * place)) * 4 + lax.rem(line + 1 + step // 2, 4)

        @pl.when(tile != me)
        def _():
            send(tile)

        return carry

    def away(step, carry):
        place = 3 - lax.rem(step, 2)
        send((place + right * (3 - 2 * place)) * 4 + lax.rem(line + 1 + step // 2, 4))
        return carry

    lax.fori_loop(0, 8, near, 0)
    lax.fori_loop(0, 8, away, 0)
    extract(me)
    parcel(me, 1 - mine, me, mine).start()
    own = pltpu.make_async_copy(outgoing.at[me, mine], arrived.at[mine, me], own_sem.at[0])
    own.start()
    own_tag = pltpu.make_async_copy(labels.at[me], arrived_labels.at[me], own_sem.at[1])
    own_tag.start()

    @pl.when(inner)
    def _():
        far_rows().wait()
        rows = pltpu.make_async_copy(far_table, far_starts, table_sem.at[2])
        rows.start()
        rows.wait()

        for pair in range(2):
            burst(0, pair).wait_recv()

            def one_tile(step, carry):
                index = lax.rem(4 * right + step, 8)

                def one(slot, carry):
                    top = far_starts[index, 0, 2 * allowance + slot]
                    proxied[index, pair, pl.ds(slot * SHARD_HEIGHT, SHARD_HEIGHT)] = halves[pair][
                        pl.ds(top, SHARD_HEIGHT)
                    ]
                    return carry

                lax.fori_loop(0, allowance, one, 0)

                @pl.when(8 * right + index != me)
                def _():
                    proxy(index, pair).start()

                @pl.when(8 * right + index == me)
                def _():
                    proxy_own(pair).start()

                return carry

            lax.fori_loop(0, 8, one_tile, 0)

    def finish(step, carry):
        tile = target_of(step)
        tag(tile, tile).wait_recv()
        tag(tile, me).wait_send()

        @pl.when(jnp.logical_or(jnp.logical_not(inner), tile != far_me))
        def _():
            parcel(tile, 1 - mine, tile, 1 - mine).wait_recv()
            parcel(tile, mine, tile, mine).wait_recv()

        @pl.when(takes(tile))
        def _():
            parcel(tile, 1 - mine, me, mine).wait_send()
            parcel(tile, mine, me, mine).wait_send()

        return carry

    lax.fori_loop(1, tile_count, finish, 0)
    parcel(me, 1 - mine, me, 1 - mine).wait_recv()
    parcel(me, 1 - mine, me, mine).wait_send()
    own.wait()
    own_tag.wait()

    @pl.when(inner)
    def _():
        def settle(index, carry):
            for pair in range(2):

                @pl.when(8 * right + index != me)
                def _():
                    proxy(index, pair).wait_send()

                @pl.when(8 * right + index == me)
                def _():
                    proxy_own(pair).wait()

            return carry

        lax.fori_loop(0, 8, settle, 0)
        for part in range(2):
            burst(part, 0).wait_send()


def combine_kernel(allowance, where, labels, arrived, spread, gather, looked, total, count, prods):
    mine = where[0]
    total[...] = jnp.zeros_like(total)
    for slot in range(SLOTS):
        count[slot] = 0

    def one_source(source, carry):
        for slot in range(allowance):
            label = labels[source, 0, slot]

            @pl.when(label > 0)
            def _():
                count[label - 1] = count[label - 1] + 1
                for part in range(2):
                    piece = arrived[part, source, pl.ds(slot * SHARD_HEIGHT, SHARD_HEIGHT)]
                    total[part, label - 1] += piece.astype(jnp.float32)

        return carry

    lax.fori_loop(0, arrived.shape[1], one_source, 0)

    def one(level, carry):
        for side in range(2):
            slot = level * 2 + side
            divisor = jnp.maximum(count[slot], 1).astype(jnp.float32)
            first = (total[1, slot] / divisor).astype(jnp.bfloat16).astype(jnp.float32)
            second = (total[0, slot] / divisor).astype(jnp.bfloat16).astype(jnp.float32)
            same = first * second
            cross = first * jnp.concatenate([second[:, 2:], second[:, :2]], axis=1)
            for kind, value in ((0, same), (1, cross)):
                boxes = [jnp.sum(value[box * LOOK_ROWS : (box + 1) * LOOK_ROWS], axis=0) for box in range(4)]
                for two in range(2):
                    at = pl.ds(pl.multiple_of((level * 2 + two) * 8, 8), 8)
                    prods[side, kind, at, :] = jnp.concatenate(boxes[2 * two : 2 * two + 2], axis=0)
        return carry

    lax.fori_loop(0, PATCH_SHARD_LEVEL, one, 0)
    sub = lax.rem(lax.broadcasted_iota(jnp.int32, (256, 128), 0), 4)
    lane = lax.broadcasted_iota(jnp.int32, (256, 128), 1)
    column = lax.rem(lane, 64)
    sign = jnp.where(jnp.logical_and(lane >= 64, sub < 2), -1.0, 1.0)
    pooled = jnp.zeros((256, 128), jnp.float32)
    for side in range(2):
        wide = jnp.dot(prods[side, 0], spread[0], precision=EXACT, preferred_element_type=jnp.float32)
        wide += jnp.dot(prods[side, 1], spread[1], precision=EXACT, preferred_element_type=jnp.float32)
        pooled += jnp.where(column // 8 == side * 4 + mine * 2 + lax.rem(sub, 2), wide * sign, 0.0)
    looked[...] = jnp.dot(gather[...], pooled, precision=EXACT, preferred_element_type=jnp.float32)


def filter_kernel(looked, left, right, right_back, out, other, send_sem, recv_sem):
    mine = lax.axis_index("pair")
    barrier = pltpu.get_barrier_semaphore()
    pl.semaphore_signal(barrier, inc=1, device_id={"pair": 1 - mine}, device_id_type=MESH)
    pl.semaphore_wait(barrier, 1)
    copy = pltpu.make_async_remote_copy(
        src_ref=looked, dst_ref=other, send_sem=send_sem, recv_sem=recv_sem,
        device_id={"pair": 1 - mine}, device_id_type=MESH,
    )
    copy.start()

    def dot(a, b):
        return jnp.dot(a, b, precision=EXACT, preferred_element_type=jnp.float32)

    length = left.shape[1]
    lane = lax.broadcasted_iota(jnp.int32, (length, 2 * length), 1)
    turn = jnp.where(lane < length, 1.0, -1.0)
    flip = jnp.where(lane < length, 1.0, 1.0 - 2.0 * mine.astype(jnp.float32))
    copy.wait()
    field = (looked[...] + other[...]) * flip
    both = dot(left[...], field)
    spectrum = both[:length] + turn * pltpu.roll(both[length:], length, 1)
    spectrum = dot(spectrum, right[...])
    power = spectrum * spectrum
    power = power + pltpu.roll(power, length, 1)
    weight = jnp.sqrt(jnp.sqrt(power + 1e-06))
    mean = jnp.sum(weight) * (1.0 / (2 * length * length))
    spectrum = spectrum * (weight / mean)
    both = dot(left[...], spectrum)
    back = both[:length] - turn * pltpu.roll(both[length:], length, 1)
    back = dot(back, right_back[...]) * (1.0 / (length * length))
    out[0] = back[:, :length]
    out[1] = back[:, length:]


def constants():
    lane = np.arange(128)
    column = np.arange(64)
    pick = (lane[:, None] // LOOK_COLS == column[None, :] % 8).astype(np.float32)
    nil = np.zeros_like(pick)
    spread = np.stack([np.concatenate([pick, nil], 1), np.concatenate([nil, pick], 1)])
    gather = (column[:, None] == np.arange(256)[None, :] // 4).astype(np.float32)
    gather = gather / (LOOK_ROWS * LOOK_COLS)
    angle = (column[:, None] * column[None, :] % 64) * (2.0 * math.pi / 64)
    cosine, sine = np.cos(angle), np.sin(angle)
    left = np.concatenate([cosine, sine], 0)
    right = np.block([[cosine, -sine], [sine, cosine]])
    right_back = np.block([[cosine, sine], [-sine, cosine]])
    return (spread, gather), tuple(x.astype(np.float32) for x in (left, right, right_back))


def local_pair(coregistered_sweeps, shard_opening_height, shard_goal_patch, shard_patch_place):
    tile_count = lax.axis_size("ground")
    piece_count = shard_opening_height.shape[0]
    allowance = max(2, (2 * piece_count + tile_count - 1) // tile_count)
    pool, transforms = constants()
    smem = pl.BlockSpec(memory_space=pltpu.SMEM)
    vmem = pl.BlockSpec(memory_space=pltpu.VMEM)
    anyplace = pl.BlockSpec(memory_space=pl.ANY)
    starts, labels = pl.pallas_call(
        functools.partial(table_kernel, allowance),
        out_shape=(
            jax.ShapeDtypeStruct((tile_count, allowance), jnp.int32),
            jax.ShapeDtypeStruct((tile_count, 1, 128), jnp.int32),
        ),
        in_specs=[smem] * 3,
        out_specs=(smem, smem),
    )(shard_opening_height, shard_goal_patch[:, 0], shard_patch_place)
    height = coregistered_sweeps.shape[2]
    sweep = (
        coregistered_sweeps[0, 0]
        .reshape(height, 2, 2, 2, 128)
        .transpose(2, 0, 1, 3, 4)
        .reshape(2, height, 4, 128)
    )
    depth = allowance * SHARD_HEIGHT
    arrived, arrived_labels = pl.pallas_call(
        functools.partial(exchange_kernel, allowance),
        out_shape=(
            jax.ShapeDtypeStruct((2, tile_count, depth, 4, 128), jnp.bfloat16),
            jax.ShapeDtypeStruct((tile_count, 1, 128), jnp.int32),
        ),
        in_specs=[smem, vmem, vmem],
        out_specs=(anyplace, vmem),
        scratch_shapes=[
            pltpu.VMEM((tile_count, 2, depth, 4, 128), jnp.bfloat16),
            pltpu.SemaphoreType.DMA((tile_count, 2)),
            pltpu.SemaphoreType.DMA((2, tile_count)),
            pltpu.SemaphoreType.DMA((tile_count,)),
            pltpu.SemaphoreType.DMA((tile_count,)),
            pltpu.SemaphoreType.DMA((2,)),
            pltpu.VMEM((height, 4, 128), jnp.bfloat16),
            pltpu.VMEM((height, 4, 128), jnp.bfloat16),
            pltpu.VMEM((8, 2, depth, 4, 128), jnp.bfloat16),
            pltpu.VMEM((8, 1, 128), jnp.int32),
            pltpu.SMEM((8, 1, 128), jnp.int32),
            pltpu.SemaphoreType.DMA((2,)),
            pltpu.SemaphoreType.DMA((2,)),
            pltpu.SemaphoreType.DMA((3,)),
            pltpu.SemaphoreType.DMA((8, 2)),
        ],
        compiler_params=pltpu.CompilerParams(
            collective_id=0, has_side_effects=True, vmem_limit_bytes=16 * 1024 * 1024
        ),
    )(starts, labels, sweep)
    where = lax.axis_index("pair").astype(jnp.int32)[None]
    looked = pl.pallas_call(
        functools.partial(combine_kernel, allowance),
        out_shape=jax.ShapeDtypeStruct((64, 128), jnp.float32),
        in_specs=[smem, smem, vmem, vmem, vmem],
        out_specs=vmem,
        scratch_shapes=[
            pltpu.VMEM((2, SLOTS, SHARD_HEIGHT, 4, 128), jnp.float32),
            pltpu.SMEM((SLOTS,), jnp.int32),
            pltpu.VMEM((2, 2, 256, 128), jnp.float32),
        ],
        compiler_params=pltpu.CompilerParams(vmem_limit_bytes=24 * 1024 * 1024),
    )(where, arrived_labels, arrived, *pool)
    filtered = pl.pallas_call(
        filter_kernel,
        out_shape=jax.ShapeDtypeStruct((2, 64, 64), jnp.float32),
        in_specs=[vmem] * 4,
        out_specs=vmem,
        scratch_shapes=[
            pltpu.VMEM((64, 128), jnp.float32),
            pltpu.SemaphoreType.DMA,
            pltpu.SemaphoreType.DMA,
        ],
        compiler_params=pltpu.CompilerParams(collective_id=1, has_side_effects=True),
    )(looked, *transforms)
    return filtered[None, None, None]


def solution(mesh):
    if mesh.shape["pair"] != 2 or mesh.shape["ground"] != 16:
        return general(mesh)
    placed = (P("pair", "ground", None, None, None), P("ground"), P("ground", None), P("ground"))
    return jax.shard_map(
        local_pair,
        mesh=mesh,
        in_specs=placed,
        out_specs=P("pair", None, "ground", None, None, None),
        check_vma=False,
    )
```

```python
import functools
import math

import jax
import jax.numpy as jnp
import numpy as np
from jax import lax
from jax.experimental import pallas as pl
from jax.experimental.pallas import tpu as pltpu
from jax.sharding import PartitionSpec as P

LOOK_ROWS = 4
LOOK_COLS = 16
SHARD_HEIGHT = 16
TILE_ROWS = 256
TILE_COLS = 1024
SWEEP_WIDTH = 512
PATCH_SHARD_LEVEL = 16
SLOTS = 32


def multilook(reference_tiles, secondary_tiles):
    first = reference_tiles.astype(jnp.float32)
    second = secondary_tiles.astype(jnp.float32)
    real_part = first[..., 0, :] * second[..., 0, :] + first[..., 1, :] * second[..., 1, :]
    imag_part = first[..., 1, :] * second[..., 0, :] - first[..., 0, :] * second[..., 1, :]
    joined = jnp.stack([real_part, imag_part], axis=-3)
    leading = joined.shape[:-2]
    row_count = joined.shape[-2]
    col_count = joined.shape[-1]
    boxes = joined.reshape(
        leading + (row_count // LOOK_ROWS, LOOK_ROWS, col_count // LOOK_COLS, LOOK_COLS)
    )
    return jnp.mean(boxes, axis=(-3, -1))


def on_left(matrix, field):
    return jnp.einsum("ij,...jk->...ik", matrix, field, precision=lax.Precision.HIGHEST)


def on_right(field, matrix):
    return jnp.einsum("...ij,jk->...ik", field, matrix, precision=lax.Precision.HIGHEST)


def goldstein(looked):
    length = looked.shape[-1]
    positions = jnp.arange(length, dtype=jnp.int32)
    phase = positions[:, None] * positions[None, :] % length
    angle = phase.astype(jnp.float32) * (2.0 * math.pi / length)
    cosine = jnp.cos(angle)
    sine = jnp.sin(angle)
    real_in = looked[..., 0, :, :]
    imag_in = looked[..., 1, :, :]
    half_real = on_left(cosine, real_in) + on_left(sine, imag_in)
    half_imag = on_left(cosine, imag_in) - on_left(sine, real_in)
    spec_real = on_right(half_real, cosine) + on_right(half_imag, sine)
    spec_imag = on_right(half_imag, cosine) - on_right(half_real, sine)
    weight = (spec_real * spec_real + spec_imag * spec_imag + 1e-06) ** 0.25
    weight = weight / jnp.mean(weight, axis=(-2, -1), keepdims=True)
    spec_real = spec_real * weight
    spec_imag = spec_imag * weight
    back_real = on_left(cosine, spec_real) - on_left(sine, spec_imag)
    back_imag = on_left(cosine, spec_imag) + on_left(sine, spec_real)
    out_real = on_right(back_real, cosine) - on_right(back_imag, sine)
    out_imag = on_right(back_imag, cosine) + on_right(back_real, sine)
    scale = 1.0 / (length * length)
    return jnp.stack([out_real * scale, out_imag * scale], axis=-3)


def partners_of(index, pair_width):
    order = jnp.arange(pair_width, dtype=jnp.int32)
    return order + (order >= index).astype(jnp.int32)


def local(coregistered_sweeps, shard_opening_height, shard_goal_patch, shard_patch_place):
    earth_patch_total_size = lax.axis_size("ground")
    pair_count = lax.axis_size("pair")
    piece_count = shard_opening_height.shape[0]
    place_allowance = max(
        2, (2 * piece_count + earth_patch_total_size - 1) // earth_patch_total_size
    )
    sweep_resident = coregistered_sweeps[0, 0]
    target = shard_goal_patch[:, 0]
    hits = (target[:, None] == jnp.arange(earth_patch_total_size, dtype=jnp.int32)[None, :]).astype(
        jnp.int32
    )
    earlier = jnp.cumsum(hits, axis=0) - hits
    rank = jnp.sum(earlier * hits, axis=1)
    position = target * place_allowance + rank
    matches = (
        position[None, :]
        == jnp.arange(earth_patch_total_size * place_allowance, dtype=jnp.int32)[:, None]
    ).astype(jnp.int32)
    tiles_filled = jnp.sum(matches, axis=1) > 0
    chosen = jnp.sum(matches * jnp.arange(piece_count, dtype=jnp.int32)[None, :], axis=1)
    sweep_height_offset = (
        shard_opening_height[chosen][:, None] + jnp.arange(SHARD_HEIGHT, dtype=jnp.int32)[None, :]
    )
    pieces_to_send = jnp.where(
        tiles_filled[:, None, None, None],
        sweep_resident[sweep_height_offset],
        jnp.zeros((), jnp.bfloat16),
    )
    labels = jnp.where(tiles_filled, shard_patch_place[chosen] + 1, 0).astype(jnp.bfloat16)
    received_pieces, arrived_labels = (
        lax.all_to_all(
            pieces_to_send.reshape(
                earth_patch_total_size, place_allowance, SHARD_HEIGHT, 2, SWEEP_WIDTH
            ),
            "ground",
            split_axis=0,
            concat_axis=0,
            tiled=True,
        ),
        lax.all_to_all(
            labels.reshape(earth_patch_total_size, place_allowance),
            "ground",
            split_axis=0,
            concat_axis=0,
            tiled=True,
        ),
    )
    pieces_flattened = received_pieces.reshape(
        earth_patch_total_size * place_allowance, SHARD_HEIGHT * 2 * SWEEP_WIDTH
    )
    slot_labels = (jnp.arange(SLOTS, dtype=jnp.int32) + 1).astype(jnp.bfloat16)
    selector = arrived_labels.reshape(-1)[None, :] == slot_labels[:, None]
    totals = jnp.dot(
        selector.astype(jnp.bfloat16), pieces_flattened, preferred_element_type=jnp.float32
    )
    counts = jnp.sum(selector.astype(jnp.float32), axis=1)
    smoothed_pixel_mean = (totals / jnp.maximum(counts, 1.0)[:, None]).astype(jnp.bfloat16)
    ground_tile = (
        smoothed_pixel_mean.reshape(PATCH_SHARD_LEVEL, 2, SHARD_HEIGHT, 2, SWEEP_WIDTH)
        .transpose(0, 2, 3, 1, 4)
        .reshape(TILE_ROWS, 2, TILE_COLS)
    )
    pair_width = pair_count - 1
    own_refs = partners_of(lax.axis_index("pair"), pair_width)
    piece = lax.all_gather(ground_tile[None], "pair", axis=0, tiled=True)
    looked_piece = multilook(piece, ground_tile[None])
    indices = jnp.arange(piece.shape[0], dtype=jnp.int32)
    selection = (own_refs[:, None] == indices[None, :]).astype(jnp.float32)
    looked = jnp.einsum("kn,nabc->kabc", selection, looked_piece, precision=lax.Precision.HIGHEST)
    return goldstein(looked)[None, :, None]


def general(mesh):
    placed = (P("pair", "ground", None, None, None), P("ground"), P("ground", None), P("ground"))
    return jax.shard_map(
        local,
        mesh=mesh,
        in_specs=placed,
        out_specs=P("pair", None, "ground", None, None, None),
        check_vma=False,
    )


MESH = pl.DeviceIdType.MESH
EXACT = lax.Precision.HIGHEST


def table_kernel(allowance, opening, goal, place, starts, labels):
    tile_count = starts.shape[0]

    def clear(tile, carry):
        for slot in range(allowance):
            starts[tile, slot] = 0
            labels[tile, 0, slot] = 0
            labels[tile, 0, 2 * allowance + slot] = 0
        labels[tile, 0, allowance] = 0
        return carry

    lax.fori_loop(0, tile_count, clear, 0)

    def enter(piece, carry):
        tile = goal[piece]
        rank = labels[tile, 0, allowance]
        starts[tile, rank] = opening[piece]
        labels[tile, 0, rank] = place[piece] + 1
        labels[tile, 0, 2 * allowance + rank] = opening[piece]
        labels[tile, 0, allowance] = rank + 1
        return carry

    lax.fori_loop(0, opening.shape[0], enter, 0)


def exchange_kernel(
    allowance, starts, labels, sweep, arrived, arrived_labels,
    outgoing, send_sem, recv_sem, label_send, label_recv, own_sem,
    first_half, second_half, proxied, far_table, far_starts, burst_send, burst_recv, table_sem, proxy_sem,
):
    me = lax.axis_index("ground")
    mine = lax.axis_index("pair")
    tile_count = 16
    level = me // 4
    line = lax.rem(me, 4)
    inner = jnp.logical_or(level == 1, level == 2)
    right = level // 2
    far = 2 - right
    barrier = pltpu.get_barrier_semaphore()

    def greet(step, carry):
        pl.semaphore_signal(
            barrier, inc=1,
            device_id={"ground": lax.rem(me + step // 2, tile_count), "pair": lax.rem(mine + step, 2)},
            device_id_type=MESH,
        )
        return carry

    lax.fori_loop(1, 2 * tile_count, greet, 0)

    def extract(tile):
        def one(slot, carry):
            top = starts[tile, slot]
            for part in range(2):
                outgoing[tile, part, pl.ds(slot * SHARD_HEIGHT, SHARD_HEIGHT)] = sweep[
                    part, pl.ds(top, SHARD_HEIGHT)
                ]
            return carry

        lax.fori_loop(0, allowance, one, 0)

    def parcel(tile, other, source, source_pair):
        return pltpu.make_async_remote_copy(
            src_ref=outgoing.at[tile, other],
            dst_ref=arrived.at[source_pair, source],
            send_sem=send_sem.at[tile, other],
            recv_sem=recv_sem.at[source_pair, source],
            device_id={"ground": tile, "pair": other},
            device_id_type=MESH,
        )

    def tag(tile, source):
        return pltpu.make_async_remote_copy(
            src_ref=labels.at[tile],
            dst_ref=arrived_labels.at[source],
            send_sem=label_send.at[tile],
            recv_sem=label_recv.at[source],
            device_id={"ground": tile, "pair": mine},
            device_id_type=MESH,
        )

    far_me = far * 4 + line

    halves = (first_half, second_half)

    def burst(part, pair):
        return pltpu.make_async_remote_copy(
            src_ref=sweep.at[part],
            dst_ref=halves[pair],
            send_sem=burst_send.at[part],
            recv_sem=burst_recv.at[pair],
            device_id={"ground": far_me, "pair": part},
            device_id_type=MESH,
        )

    def far_rows():
        return pltpu.make_async_remote_copy(
            src_ref=labels.at[pl.ds(8 * (1 - right), 8)],
            dst_ref=far_table,
            send_sem=table_sem.at[0],
            recv_sem=table_sem.at[1],
            device_id={"ground": far_me, "pair": mine},
            device_id_type=MESH,
        )

    def proxy(index, pair):
        return pltpu.make_async_remote_copy(
            src_ref=proxied.at[index, pair],
            dst_ref=arrived.at[pair, far_me],
            send_sem=proxy_sem.at[index, pair],
            recv_sem=recv_sem.at[pair, far_me],
            device_id={"ground": 8 * right + index, "pair": mine},
            device_id_type=MESH,
        )

    def proxy_own(pair):
        index = me - 8 * right
        return pltpu.make_async_copy(
            proxied.at[index, pair], arrived.at[pair, far_me], proxy_sem.at[index, pair]
        )

    def target_of(step):
        return lax.rem(me + step, tile_count)

    def takes(tile):
        return jnp.logical_or(jnp.logical_not(inner), tile // 8 == right)

    def send(tile):
        tag(tile, me).start()

        @pl.when(takes(tile))
        def _():
            extract(tile)
            parcel(tile, 1 - mine, me, mine).start()
            parcel(tile, mine, me, mine).start()

    pl.semaphore_wait(barrier, 2 * tile_count - 1)

    @pl.when(inner)
    def _():
        far_rows().start()
        for pair in range(2):

            @pl.when(mine == pair)
            def _():
                for part in (pair, 1 - pair):
                    burst(part, pair).start()

    mirror = level + right * (3 - 2 * level)

    def near(step, carry):
        distance = 1 - lax.rem(step, 2)
        place = distance + mirror - 2 * distance * mirror
        tile = (place + right * (3 - 2 * place)) * 4 + lax.rem(line + 1 + step // 2, 4)

        @pl.when(tile != me)
        def _():
            send(tile)

        return carry

    def away(step, carry):
        place = 3 - lax.rem(step, 2)
        send((place + right * (3 - 2 * place)) * 4 + lax.rem(line + 1 + step // 2, 4))
        return carry

    lax.fori_loop(0, 8, near, 0)
    lax.fori_loop(0, 8, away, 0)
    extract(me)
    parcel(me, 1 - mine, me, mine).start()
    own = pltpu.make_async_copy(outgoing.at[me, mine], arrived.at[mine, me], own_sem.at[0])
    own.start()
    own_tag = pltpu.make_async_copy(labels.at[me], arrived_labels.at[me], own_sem.at[1])
    own_tag.start()

    @pl.when(inner)
    def _():
        far_rows().wait()
        rows = pltpu.make_async_copy(far_table, far_starts, table_sem.at[2])
        rows.start()
        rows.wait()

        def serve(pair):
            burst(0, pair).wait_recv()

            def one_tile(step, carry):
                index = lax.rem(4 * right + step, 8)

                def one(slot, carry):
                    top = far_starts[index, 0, 2 * allowance + slot]
                    proxied[index, pair, pl.ds(slot * SHARD_HEIGHT, SHARD_HEIGHT)] = halves[pair][
                        pl.ds(top, SHARD_HEIGHT)
                    ]
                    return carry

                lax.fori_loop(0, allowance, one, 0)

                @pl.when(8 * right + index != me)
                def _():
                    proxy(index, pair).start()

                @pl.when(8 * right + index == me)
                def _():
                    proxy_own(pair).start()

                return carry

            lax.fori_loop(0, 8, one_tile, 0)

        for first in range(2):

            @pl.when(mine == first)
            def _():
                serve(first)
                serve(1 - first)

    def finish(step, carry):
        tile = target_of(step)
        tag(tile, tile).wait_recv()
        tag(tile, me).wait_send()

        @pl.when(jnp.logical_or(jnp.logical_not(inner), tile != far_me))
        def _():
            parcel(tile, 1 - mine, tile, 1 - mine).wait_recv()
            parcel(tile, mine, tile, mine).wait_recv()

        @pl.when(takes(tile))
        def _():
            parcel(tile, 1 - mine, me, mine).wait_send()
            parcel(tile, mine, me, mine).wait_send()

        return carry

    lax.fori_loop(1, tile_count, finish, 0)
    parcel(me, 1 - mine, me, 1 - mine).wait_recv()
    parcel(me, 1 - mine, me, mine).wait_send()
    own.wait()
    own_tag.wait()

    @pl.when(inner)
    def _():
        def settle(index, carry):
            for pair in range(2):

                @pl.when(8 * right + index != me)
                def _():
                    proxy(index, pair).wait_send()

                @pl.when(8 * right + index == me)
                def _():
                    proxy_own(pair).wait()

            return carry

        lax.fori_loop(0, 8, settle, 0)
        for part in range(2):
            burst(part, 0).wait_send()


def combine_kernel(allowance, labels, arrived, spread, gather, looked, total, count, prods):
    mine = lax.axis_index("pair")
    total[...] = jnp.zeros_like(total)
    for slot in range(SLOTS):
        count[slot] = 0

    def one_source(source, carry):
        for slot in range(allowance):
            label = labels[source, 0, slot]

            @pl.when(label > 0)
            def _():
                count[label - 1] = count[label - 1] + 1
                for part in range(2):
                    piece = arrived[part, source, pl.ds(slot * SHARD_HEIGHT, SHARD_HEIGHT)]
                    total[part, label - 1] += piece.astype(jnp.float32)

        return carry

    lax.fori_loop(0, arrived.shape[1], one_source, 0)

    def one(level, carry):
        for side in range(2):
            slot = level * 2 + side
            divisor = jnp.maximum(count[slot], 1).astype(jnp.float32)
            first = (total[1, slot] / divisor).astype(jnp.bfloat16).astype(jnp.float32)
            second = (total[0, slot] / divisor).astype(jnp.bfloat16).astype(jnp.float32)
            same = first * second
            cross = first * jnp.concatenate([second[:, 2:], second[:, :2]], axis=1)
            for kind, value in ((0, same), (1, cross)):
                boxes = [jnp.sum(value[box * LOOK_ROWS : (box + 1) * LOOK_ROWS], axis=0) for box in range(4)]
                for two in range(2):
                    at = pl.ds(pl.multiple_of((level * 2 + two) * 8, 8), 8)
                    prods[side, kind, at, :] = jnp.concatenate(boxes[2 * two : 2 * two + 2], axis=0)
        return carry

    lax.fori_loop(0, PATCH_SHARD_LEVEL, one, 0)
    sub = lax.rem(lax.broadcasted_iota(jnp.int32, (256, 128), 0), 4)
    lane = lax.broadcasted_iota(jnp.int32, (256, 128), 1)
    column = lax.rem(lane, 64)
    sign = jnp.where(jnp.logical_and(lane >= 64, sub < 2), -1.0, 1.0)
    pooled = jnp.zeros((256, 128), jnp.float32)
    for side in range(2):
        wide = jnp.dot(prods[side, 0], spread[0], precision=EXACT, preferred_element_type=jnp.float32)
        wide += jnp.dot(prods[side, 1], spread[1], precision=EXACT, preferred_element_type=jnp.float32)
        pooled += jnp.where(column // 8 == side * 4 + mine * 2 + lax.rem(sub, 2), wide * sign, 0.0)
    looked[...] = jnp.dot(gather[...], pooled, precision=EXACT, preferred_element_type=jnp.float32)


def filter_kernel(looked, left, right, right_back, out, other, send_sem, recv_sem):
    mine = lax.axis_index("pair")
    barrier = pltpu.get_barrier_semaphore()
    pl.semaphore_signal(barrier, inc=1, device_id={"pair": 1 - mine}, device_id_type=MESH)
    pl.semaphore_wait(barrier, 1)
    copy = pltpu.make_async_remote_copy(
        src_ref=looked, dst_ref=other, send_sem=send_sem, recv_sem=recv_sem,
        device_id={"pair": 1 - mine}, device_id_type=MESH,
    )
    copy.start()

    def dot(a, b):
        return jnp.dot(a, b, precision=EXACT, preferred_element_type=jnp.float32)

    length = left.shape[1]
    lane = lax.broadcasted_iota(jnp.int32, (length, 2 * length), 1)
    turn = jnp.where(lane < length, 1.0, -1.0)
    flip = jnp.where(lane < length, 1.0, 1.0 - 2.0 * mine.astype(jnp.float32))
    copy.wait()
    field = (looked[...] + other[...]) * flip
    both = dot(left[...], field)
    spectrum = both[:length] + turn * pltpu.roll(both[length:], length, 1)
    spectrum = dot(spectrum, right[...])
    power = spectrum * spectrum
    power = power + pltpu.roll(power, length, 1)
    weight = jnp.sqrt(jnp.sqrt(power + 1e-06))
    mean = jnp.sum(weight) * (1.0 / (2 * length * length))
    spectrum = spectrum * (weight / mean)
    both = dot(left[...], spectrum)
    back = both[:length] - turn * pltpu.roll(both[length:], length, 1)
    back = dot(back, right_back[...]) * (1.0 / (length * length))
    out[0] = back[:, :length]
    out[1] = back[:, length:]


def constants():
    lane = np.arange(128)
    column = np.arange(64)
    pick = (lane[:, None] // LOOK_COLS == column[None, :] % 8).astype(np.float32)
    nil = np.zeros_like(pick)
    spread = np.stack([np.concatenate([pick, nil], 1), np.concatenate([nil, pick], 1)])
    gather = (column[:, None] == np.arange(256)[None, :] // 4).astype(np.float32)
    gather = gather / (LOOK_ROWS * LOOK_COLS)
    angle = (column[:, None] * column[None, :] % 64) * (2.0 * math.pi / 64)
    cosine, sine = np.cos(angle), np.sin(angle)
    left = np.concatenate([cosine, sine], 0)
    right = np.block([[cosine, -sine], [sine, cosine]])
    right_back = np.block([[cosine, sine], [-sine, cosine]])
    return (spread, gather), tuple(x.astype(np.float32) for x in (left, right, right_back))


def local_pair(coregistered_sweeps, shard_opening_height, shard_goal_patch, shard_patch_place):
    tile_count = lax.axis_size("ground")
    piece_count = shard_opening_height.shape[0]
    allowance = max(2, (2 * piece_count + tile_count - 1) // tile_count)
    pool, transforms = constants()
    smem = pl.BlockSpec(memory_space=pltpu.SMEM)
    vmem = pl.BlockSpec(memory_space=pltpu.VMEM)
    anyplace = pl.BlockSpec(memory_space=pl.ANY)
    starts, labels = pl.pallas_call(
        functools.partial(table_kernel, allowance),
        out_shape=(
            jax.ShapeDtypeStruct((tile_count, allowance), jnp.int32),
            jax.ShapeDtypeStruct((tile_count, 1, 128), jnp.int32),
        ),
        in_specs=[smem] * 3,
        out_specs=(smem, smem),
    )(shard_opening_height, shard_goal_patch[:, 0], shard_patch_place)
    height = coregistered_sweeps.shape[2]
    sweep = (
        coregistered_sweeps[0, 0]
        .reshape(height, 2, 2, 2, 128)
        .transpose(2, 0, 1, 3, 4)
        .reshape(2, height, 4, 128)
    )
    depth = allowance * SHARD_HEIGHT
    arrived, arrived_labels = pl.pallas_call(
        functools.partial(exchange_kernel, allowance),
        out_shape=(
            jax.ShapeDtypeStruct((2, tile_count, depth, 4, 128), jnp.bfloat16),
            jax.ShapeDtypeStruct((tile_count, 1, 128), jnp.int32),
        ),
        in_specs=[smem, vmem, vmem],
        out_specs=(anyplace, vmem),
        scratch_shapes=[
            pltpu.VMEM((tile_count, 2, depth, 4, 128), jnp.bfloat16),
            pltpu.SemaphoreType.DMA((tile_count, 2)),
            pltpu.SemaphoreType.DMA((2, tile_count)),
            pltpu.SemaphoreType.DMA((tile_count,)),
            pltpu.SemaphoreType.DMA((tile_count,)),
            pltpu.SemaphoreType.DMA((2,)),
            pltpu.VMEM((height, 4, 128), jnp.bfloat16),
            pltpu.VMEM((height, 4, 128), jnp.bfloat16),
            pltpu.VMEM((8, 2, depth, 4, 128), jnp.bfloat16),
            pltpu.VMEM((8, 1, 128), jnp.int32),
            pltpu.SMEM((8, 1, 128), jnp.int32),
            pltpu.SemaphoreType.DMA((2,)),
            pltpu.SemaphoreType.DMA((2,)),
            pltpu.SemaphoreType.DMA((3,)),
            pltpu.SemaphoreType.DMA((8, 2)),
        ],
        compiler_params=pltpu.CompilerParams(
            collective_id=0, has_side_effects=True, vmem_limit_bytes=9 * 1024 * 1024
        ),
    )(starts, labels, sweep)
    looked = pl.pallas_call(
        functools.partial(combine_kernel, allowance),
        out_shape=jax.ShapeDtypeStruct((64, 128), jnp.float32),
        in_specs=[smem, vmem, vmem, vmem],
        out_specs=vmem,
        scratch_shapes=[
            pltpu.VMEM((2, SLOTS, SHARD_HEIGHT, 4, 128), jnp.float32),
            pltpu.SMEM((SLOTS,), jnp.int32),
            pltpu.VMEM((2, 2, 256, 128), jnp.float32),
        ],
        compiler_params=pltpu.CompilerParams(vmem_limit_bytes=12 * 1024 * 1024),
    )(arrived_labels, arrived, *pool)
    filtered = pl.pallas_call(
        filter_kernel,
        out_shape=jax.ShapeDtypeStruct((2, 64, 64), jnp.float32),
        in_specs=[vmem] * 4,
        out_specs=vmem,
        scratch_shapes=[
            pltpu.VMEM((64, 128), jnp.float32),
            pltpu.SemaphoreType.DMA,
            pltpu.SemaphoreType.DMA,
        ],
        compiler_params=pltpu.CompilerParams(collective_id=1, has_side_effects=True),
    )(looked, *transforms)
    return filtered[None, None, None]


def solution(mesh):
    if mesh.shape["pair"] != 2 or mesh.shape["ground"] != 16:
        return general(mesh)
    placed = (P("pair", "ground", None, None, None), P("ground"), P("ground", None), P("ground"))
    return jax.shard_map(
        local_pair,
        mesh=mesh,
        in_specs=placed,
        out_specs=P("pair", None, "ground", None, None, None),
        check_vma=False,
    )
```

```python
import functools
import math

import jax
import jax.numpy as jnp
import numpy as np
from jax import lax
from jax.experimental import pallas as pl
from jax.experimental.pallas import tpu as pltpu
from jax.sharding import PartitionSpec as P

LOOK_ROWS = 4
LOOK_COLS = 16
SHARD_HEIGHT = 16
TILE_ROWS = 256
TILE_COLS = 1024
SWEEP_WIDTH = 512
PATCH_SHARD_LEVEL = 16
SLOTS = 32


def multilook(reference_tiles, secondary_tiles):
    first = reference_tiles.astype(jnp.float32)
    second = secondary_tiles.astype(jnp.float32)
    real_part = first[..., 0, :] * second[..., 0, :] + first[..., 1, :] * second[..., 1, :]
    imag_part = first[..., 1, :] * second[..., 0, :] - first[..., 0, :] * second[..., 1, :]
    joined = jnp.stack([real_part, imag_part], axis=-3)
    leading = joined.shape[:-2]
    row_count = joined.shape[-2]
    col_count = joined.shape[-1]
    boxes = joined.reshape(
        leading + (row_count // LOOK_ROWS, LOOK_ROWS, col_count // LOOK_COLS, LOOK_COLS)
    )
    return jnp.mean(boxes, axis=(-3, -1))


def on_left(matrix, field):
    return jnp.einsum("ij,...jk->...ik", matrix, field, precision=lax.Precision.HIGHEST)


def on_right(field, matrix):
    return jnp.einsum("...ij,jk->...ik", field, matrix, precision=lax.Precision.HIGHEST)


def goldstein(looked):
    length = looked.shape[-1]
    positions = jnp.arange(length, dtype=jnp.int32)
    phase = positions[:, None] * positions[None, :] % length
    angle = phase.astype(jnp.float32) * (2.0 * math.pi / length)
    cosine = jnp.cos(angle)
    sine = jnp.sin(angle)
    real_in = looked[..., 0, :, :]
    imag_in = looked[..., 1, :, :]
    half_real = on_left(cosine, real_in) + on_left(sine, imag_in)
    half_imag = on_left(cosine, imag_in) - on_left(sine, real_in)
    spec_real = on_right(half_real, cosine) + on_right(half_imag, sine)
    spec_imag = on_right(half_imag, cosine) - on_right(half_real, sine)
    weight = (spec_real * spec_real + spec_imag * spec_imag + 1e-06) ** 0.25
    weight = weight / jnp.mean(weight, axis=(-2, -1), keepdims=True)
    spec_real = spec_real * weight
    spec_imag = spec_imag * weight
    back_real = on_left(cosine, spec_real) - on_left(sine, spec_imag)
    back_imag = on_left(cosine, spec_imag) + on_left(sine, spec_real)
    out_real = on_right(back_real, cosine) - on_right(back_imag, sine)
    out_imag = on_right(back_imag, cosine) + on_right(back_real, sine)
    scale = 1.0 / (length * length)
    return jnp.stack([out_real * scale, out_imag * scale], axis=-3)


def partners_of(index, pair_width):
    order = jnp.arange(pair_width, dtype=jnp.int32)
    return order + (order >= index).astype(jnp.int32)


def local(coregistered_sweeps, shard_opening_height, shard_goal_patch, shard_patch_place):
    earth_patch_total_size = lax.axis_size("ground")
    pair_count = lax.axis_size("pair")
    piece_count = shard_opening_height.shape[0]
    place_allowance = max(
        2, (2 * piece_count + earth_patch_total_size - 1) // earth_patch_total_size
    )
    sweep_resident = coregistered_sweeps[0, 0]
    target = shard_goal_patch[:, 0]
    hits = (target[:, None] == jnp.arange(earth_patch_total_size, dtype=jnp.int32)[None, :]).astype(
        jnp.int32
    )
    earlier = jnp.cumsum(hits, axis=0) - hits
    rank = jnp.sum(earlier * hits, axis=1)
    position = target * place_allowance + rank
    matches = (
        position[None, :]
        == jnp.arange(earth_patch_total_size * place_allowance, dtype=jnp.int32)[:, None]
    ).astype(jnp.int32)
    tiles_filled = jnp.sum(matches, axis=1) > 0
    chosen = jnp.sum(matches * jnp.arange(piece_count, dtype=jnp.int32)[None, :], axis=1)
    sweep_height_offset = (
        shard_opening_height[chosen][:, None] + jnp.arange(SHARD_HEIGHT, dtype=jnp.int32)[None, :]
    )
    pieces_to_send = jnp.where(
        tiles_filled[:, None, None, None],
        sweep_resident[sweep_height_offset],
        jnp.zeros((), jnp.bfloat16),
    )
    labels = jnp.where(tiles_filled, shard_patch_place[chosen] + 1, 0).astype(jnp.bfloat16)
    received_pieces, arrived_labels = (
        lax.all_to_all(
            pieces_to_send.reshape(
                earth_patch_total_size, place_allowance, SHARD_HEIGHT, 2, SWEEP_WIDTH
            ),
            "ground",
            split_axis=0,
            concat_axis=0,
            tiled=True,
        ),
        lax.all_to_all(
            labels.reshape(earth_patch_total_size, place_allowance),
            "ground",
            split_axis=0,
            concat_axis=0,
            tiled=True,
        ),
    )
    pieces_flattened = received_pieces.reshape(
        earth_patch_total_size * place_allowance, SHARD_HEIGHT * 2 * SWEEP_WIDTH
    )
    slot_labels = (jnp.arange(SLOTS, dtype=jnp.int32) + 1).astype(jnp.bfloat16)
    selector = arrived_labels.reshape(-1)[None, :] == slot_labels[:, None]
    totals = jnp.dot(
        selector.astype(jnp.bfloat16), pieces_flattened, preferred_element_type=jnp.float32
    )
    counts = jnp.sum(selector.astype(jnp.float32), axis=1)
    smoothed_pixel_mean = (totals / jnp.maximum(counts, 1.0)[:, None]).astype(jnp.bfloat16)
    ground_tile = (
        smoothed_pixel_mean.reshape(PATCH_SHARD_LEVEL, 2, SHARD_HEIGHT, 2, SWEEP_WIDTH)
        .transpose(0, 2, 3, 1, 4)
        .reshape(TILE_ROWS, 2, TILE_COLS)
    )
    pair_width = pair_count - 1
    own_refs = partners_of(lax.axis_index("pair"), pair_width)
    piece = lax.all_gather(ground_tile[None], "pair", axis=0, tiled=True)
    looked_piece = multilook(piece, ground_tile[None])
    indices = jnp.arange(piece.shape[0], dtype=jnp.int32)
    selection = (own_refs[:, None] == indices[None, :]).astype(jnp.float32)
    looked = jnp.einsum("kn,nabc->kabc", selection, looked_piece, precision=lax.Precision.HIGHEST)
    return goldstein(looked)[None, :, None]


def general(mesh):
    placed = (P("pair", "ground", None, None, None), P("ground"), P("ground", None), P("ground"))
    return jax.shard_map(
        local,
        mesh=mesh,
        in_specs=placed,
        out_specs=P("pair", None, "ground", None, None, None),
        check_vma=False,
    )


CHUNKS = 8
MESH = pl.DeviceIdType.MESH
EXACT = lax.Precision.HIGHEST


def table_kernel(allowance, opening, goal, place, starts, labels):
    tile_count = starts.shape[0]

    def clear(tile, carry):
        for slot in range(allowance):
            starts[tile, slot] = 0
            labels[tile, 0, slot] = 0
            labels[tile, 0, 2 * allowance + slot] = 0
        labels[tile, 0, allowance] = 0
        return carry

    lax.fori_loop(0, tile_count, clear, 0)

    def enter(piece, carry):
        tile = goal[piece]
        rank = labels[tile, 0, allowance]
        starts[tile, rank] = opening[piece]
        labels[tile, 0, rank] = place[piece] + 1
        labels[tile, 0, 2 * allowance + rank] = opening[piece]
        labels[tile, 0, allowance] = rank + 1
        return carry

    lax.fori_loop(0, opening.shape[0], enter, 0)


def exchange_kernel(
    allowance, starts, labels, sweep, arrived, arrived_labels,
    outgoing, send_sem, recv_sem, label_send, label_recv, own_sem,
    first_half, second_half, proxied, far_table, far_starts, burst_send, burst_recv, table_sem, proxy_sem,
):
    me = lax.axis_index("ground")
    mine = lax.axis_index("pair")
    tile_count = 16
    level = me // 4
    line = lax.rem(me, 4)
    inner = jnp.logical_or(level == 1, level == 2)
    right = level // 2
    far = 2 - right
    barrier = pltpu.get_barrier_semaphore()

    def greet(step, carry):
        pl.semaphore_signal(
            barrier, inc=1,
            device_id={"ground": lax.rem(me + step // 2, tile_count), "pair": lax.rem(mine + step, 2)},
            device_id_type=MESH,
        )
        return carry

    lax.fori_loop(1, 2 * tile_count, greet, 0)

    def extract(tile):
        def one(slot, carry):
            top = starts[tile, slot]
            for part in range(2):
                outgoing[tile, part, pl.ds(slot * SHARD_HEIGHT, SHARD_HEIGHT)] = sweep[
                    part, pl.ds(top, SHARD_HEIGHT)
                ]
            return carry

        lax.fori_loop(0, allowance, one, 0)

    def parcel(tile, other, source, source_pair):
        return pltpu.make_async_remote_copy(
            src_ref=outgoing.at[tile, other],
            dst_ref=arrived.at[source_pair, source],
            send_sem=send_sem.at[tile, other],
            recv_sem=recv_sem.at[source_pair, source],
            device_id={"ground": tile, "pair": other},
            device_id_type=MESH,
        )

    def tag(tile, source):
        return pltpu.make_async_remote_copy(
            src_ref=labels.at[tile],
            dst_ref=arrived_labels.at[source],
            send_sem=label_send.at[tile],
            recv_sem=label_recv.at[source],
            device_id={"ground": tile, "pair": mine},
            device_id_type=MESH,
        )

    far_me = far * 4 + line

    halves = (first_half, second_half)

    span = sweep.shape[1] // CHUNKS

    def burst(part, pair, chunk):
        rows = pl.ds(chunk * span, span)
        return pltpu.make_async_remote_copy(
            src_ref=sweep.at[part, rows],
            dst_ref=halves[pair].at[rows],
            send_sem=burst_send.at[part, chunk],
            recv_sem=burst_recv.at[pair, chunk],
            device_id={"ground": far_me, "pair": part},
            device_id_type=MESH,
        )

    def far_rows():
        return pltpu.make_async_remote_copy(
            src_ref=labels.at[pl.ds(8 * (1 - right), 8)],
            dst_ref=far_table,
            send_sem=table_sem.at[0],
            recv_sem=table_sem.at[1],
            device_id={"ground": far_me, "pair": mine},
            device_id_type=MESH,
        )

    def proxy(index, pair):
        return pltpu.make_async_remote_copy(
            src_ref=proxied.at[index, pair],
            dst_ref=arrived.at[pair, far_me],
            send_sem=proxy_sem.at[index, pair],
            recv_sem=recv_sem.at[pair, far_me],
            device_id={"ground": 8 * right + index, "pair": mine},
            device_id_type=MESH,
        )

    def proxy_own(pair):
        index = me - 8 * right
        return pltpu.make_async_copy(
            proxied.at[index, pair], arrived.at[pair, far_me], proxy_sem.at[index, pair]
        )

    def target_of(step):
        return lax.rem(me + step, tile_count)

    def takes(tile):
        return jnp.logical_or(jnp.logical_not(inner), tile // 8 == right)

    def send(tile):
        tag(tile, me).start()

        @pl.when(takes(tile))
        def _():
            extract(tile)
            parcel(tile, 1 - mine, me, mine).start()
            parcel(tile, mine, me, mine).start()

    pl.semaphore_wait(barrier, 2 * tile_count - 1)

    @pl.when(inner)
    def _():
        far_rows().start()
        for pair in range(2):

            @pl.when(mine == pair)
            def _():
                for part in (pair, 1 - pair):
                    for chunk in range(CHUNKS):
                        burst(part, pair, chunk).start()

    mirror = level + right * (3 - 2 * level)

    def near(step, carry):
        distance = 1 - lax.rem(step, 2)
        place = distance + mirror - 2 * distance * mirror
        tile = (place + right * (3 - 2 * place)) * 4 + lax.rem(line + 1 + step // 2, 4)

        @pl.when(tile != me)
        def _():
            send(tile)

        return carry

    def away(step, carry):
        place = 3 - lax.rem(step, 2)
        send((place + right * (3 - 2 * place)) * 4 + lax.rem(line + 1 + step // 2, 4))
        return carry

    lax.fori_loop(0, 8, near, 0)
    lax.fori_loop(0, 8, away, 0)
    extract(me)
    parcel(me, 1 - mine, me, mine).start()
    own = pltpu.make_async_copy(outgoing.at[me, mine], arrived.at[mine, me], own_sem.at[0])
    own.start()
    own_tag = pltpu.make_async_copy(labels.at[me], arrived_labels.at[me], own_sem.at[1])
    own_tag.start()

    @pl.when(inner)
    def _():
        far_rows().wait()
        rows = pltpu.make_async_copy(far_table, far_starts, table_sem.at[2])
        rows.start()
        rows.wait()

        def serve(pair):
            for chunk in range(CHUNKS):
                burst(0, pair, chunk).wait_recv()

            def one_tile(step, carry):
                index = lax.rem(4 * right + step, 8)

                def one(slot, carry):
                    top = far_starts[index, 0, 2 * allowance + slot]
                    proxied[index, pair, pl.ds(slot * SHARD_HEIGHT, SHARD_HEIGHT)] = halves[pair][
                        pl.ds(top, SHARD_HEIGHT)
                    ]
                    return carry

                lax.fori_loop(0, allowance, one, 0)

                @pl.when(8 * right + index != me)
                def _():
                    proxy(index, pair).start()

                @pl.when(8 * right + index == me)
                def _():
                    proxy_own(pair).start()

                return carry

            lax.fori_loop(0, 8, one_tile, 0)

        for first in range(2):

            @pl.when(mine == first)
            def _():
                serve(first)
                serve(1 - first)

    def finish(step, carry):
        tile = target_of(step)
        tag(tile, tile).wait_recv()
        tag(tile, me).wait_send()

        @pl.when(jnp.logical_or(jnp.logical_not(inner), tile != far_me))
        def _():
            parcel(tile, 1 - mine, tile, 1 - mine).wait_recv()
            parcel(tile, mine, tile, mine).wait_recv()

        @pl.when(takes(tile))
        def _():
            parcel(tile, 1 - mine, me, mine).wait_send()
            parcel(tile, mine, me, mine).wait_send()

        return carry

    lax.fori_loop(1, tile_count, finish, 0)
    parcel(me, 1 - mine, me, 1 - mine).wait_recv()
    parcel(me, 1 - mine, me, mine).wait_send()
    own.wait()
    own_tag.wait()

    @pl.when(inner)
    def _():
        def settle(index, carry):
            for pair in range(2):

                @pl.when(8 * right + index != me)
                def _():
                    proxy(index, pair).wait_send()

                @pl.when(8 * right + index == me)
                def _():
                    proxy_own(pair).wait()

            return carry

        lax.fori_loop(0, 8, settle, 0)
        for part in range(2):
            for chunk in range(CHUNKS):
                burst(part, 0, chunk).wait_send()


def combine_kernel(allowance, labels, arrived, spread, gather, looked, total, count, prods):
    mine = lax.axis_index("pair")
    total[...] = jnp.zeros_like(total)
    for slot in range(SLOTS):
        count[slot] = 0

    def one_source(source, carry):
        for slot in range(allowance):
            label = labels[source, 0, slot]

            @pl.when(label > 0)
            def _():
                count[label - 1] = count[label - 1] + 1
                for part in range(2):
                    piece = arrived[part, source, pl.ds(slot * SHARD_HEIGHT, SHARD_HEIGHT)]
                    total[part, label - 1] += piece.astype(jnp.float32)

        return carry

    lax.fori_loop(0, arrived.shape[1], one_source, 0)

    def one(level, carry):
        for side in range(2):
            slot = level * 2 + side
            divisor = jnp.maximum(count[slot], 1).astype(jnp.float32)
            first = (total[1, slot] / divisor).astype(jnp.bfloat16).astype(jnp.float32)
            second = (total[0, slot] / divisor).astype(jnp.bfloat16).astype(jnp.float32)
            same = first * second
            cross = first * jnp.concatenate([second[:, 2:], second[:, :2]], axis=1)
            for kind, value in ((0, same), (1, cross)):
                boxes = [jnp.sum(value[box * LOOK_ROWS : (box + 1) * LOOK_ROWS], axis=0) for box in range(4)]
                for two in range(2):
                    at = pl.ds(pl.multiple_of((level * 2 + two) * 8, 8), 8)
                    prods[side, kind, at, :] = jnp.concatenate(boxes[2 * two : 2 * two + 2], axis=0)
        return carry

    lax.fori_loop(0, PATCH_SHARD_LEVEL, one, 0)
    sub = lax.rem(lax.broadcasted_iota(jnp.int32, (256, 128), 0), 4)
    lane = lax.broadcasted_iota(jnp.int32, (256, 128), 1)
    column = lax.rem(lane, 64)
    sign = jnp.where(jnp.logical_and(lane >= 64, sub < 2), -1.0, 1.0)
    pooled = jnp.zeros((256, 128), jnp.float32)
    for side in range(2):
        wide = jnp.dot(prods[side, 0], spread[0], precision=EXACT, preferred_element_type=jnp.float32)
        wide += jnp.dot(prods[side, 1], spread[1], precision=EXACT, preferred_element_type=jnp.float32)
        pooled += jnp.where(column // 8 == side * 4 + mine * 2 + lax.rem(sub, 2), wide * sign, 0.0)
    looked[...] = jnp.dot(gather[...], pooled, precision=EXACT, preferred_element_type=jnp.float32)


def filter_kernel(looked, left, right, right_back, out, other, send_sem, recv_sem):
    mine = lax.axis_index("pair")
    barrier = pltpu.get_barrier_semaphore()
    pl.semaphore_signal(barrier, inc=1, device_id={"pair": 1 - mine}, device_id_type=MESH)
    pl.semaphore_wait(barrier, 1)
    copy = pltpu.make_async_remote_copy(
        src_ref=looked, dst_ref=other, send_sem=send_sem, recv_sem=recv_sem,
        device_id={"pair": 1 - mine}, device_id_type=MESH,
    )
    copy.start()

    def dot(a, b):
        return jnp.dot(a, b, precision=EXACT, preferred_element_type=jnp.float32)

    length = left.shape[1]
    lane = lax.broadcasted_iota(jnp.int32, (length, 2 * length), 1)
    turn = jnp.where(lane < length, 1.0, -1.0)
    flip = jnp.where(lane < length, 1.0, 1.0 - 2.0 * mine.astype(jnp.float32))
    copy.wait()
    field = (looked[...] + other[...]) * flip
    both = dot(left[...], field)
    spectrum = both[:length] + turn * pltpu.roll(both[length:], length, 1)
    spectrum = dot(spectrum, right[...])
    power = spectrum * spectrum
    power = power + pltpu.roll(power, length, 1)
    weight = jnp.sqrt(jnp.sqrt(power + 1e-06))
    mean = jnp.sum(weight) * (1.0 / (2 * length * length))
    spectrum = spectrum * (weight / mean)
    both = dot(left[...], spectrum)
    back = both[:length] - turn * pltpu.roll(both[length:], length, 1)
    back = dot(back, right_back[...]) * (1.0 / (length * length))
    out[0] = back[:, :length]
    out[1] = back[:, length:]


def constants():
    lane = np.arange(128)
    column = np.arange(64)
    pick = (lane[:, None] // LOOK_COLS == column[None, :] % 8).astype(np.float32)
    nil = np.zeros_like(pick)
    spread = np.stack([np.concatenate([pick, nil], 1), np.concatenate([nil, pick], 1)])
    gather = (column[:, None] == np.arange(256)[None, :] // 4).astype(np.float32)
    gather = gather / (LOOK_ROWS * LOOK_COLS)
    angle = (column[:, None] * column[None, :] % 64) * (2.0 * math.pi / 64)
    cosine, sine = np.cos(angle), np.sin(angle)
    left = np.concatenate([cosine, sine], 0)
    right = np.block([[cosine, -sine], [sine, cosine]])
    right_back = np.block([[cosine, sine], [-sine, cosine]])
    return (spread, gather), tuple(x.astype(np.float32) for x in (left, right, right_back))


def local_pair(coregistered_sweeps, shard_opening_height, shard_goal_patch, shard_patch_place):
    tile_count = lax.axis_size("ground")
    piece_count = shard_opening_height.shape[0]
    allowance = max(2, (2 * piece_count + tile_count - 1) // tile_count)
    pool, transforms = constants()
    smem = pl.BlockSpec(memory_space=pltpu.SMEM)
    vmem = pl.BlockSpec(memory_space=pltpu.VMEM)
    anyplace = pl.BlockSpec(memory_space=pl.ANY)
    starts, labels = pl.pallas_call(
        functools.partial(table_kernel, allowance),
        out_shape=(
            jax.ShapeDtypeStruct((tile_count, allowance), jnp.int32),
            jax.ShapeDtypeStruct((tile_count, 1, 128), jnp.int32),
        ),
        in_specs=[smem] * 3,
        out_specs=(smem, smem),
    )(shard_opening_height, shard_goal_patch[:, 0], shard_patch_place)
    height = coregistered_sweeps.shape[2]
    sweep = (
        coregistered_sweeps[0, 0]
        .reshape(height, 2, 2, 2, 128)
        .transpose(2, 0, 1, 3, 4)
        .reshape(2, height, 4, 128)
    )
    depth = allowance * SHARD_HEIGHT
    arrived, arrived_labels = pl.pallas_call(
        functools.partial(exchange_kernel, allowance),
        out_shape=(
            jax.ShapeDtypeStruct((2, tile_count, depth, 4, 128), jnp.bfloat16),
            jax.ShapeDtypeStruct((tile_count, 1, 128), jnp.int32),
        ),
        in_specs=[smem, vmem, vmem],
        out_specs=(anyplace, vmem),
        scratch_shapes=[
            pltpu.VMEM((tile_count, 2, depth, 4, 128), jnp.bfloat16),
            pltpu.SemaphoreType.DMA((tile_count, 2)),
            pltpu.SemaphoreType.DMA((2, tile_count)),
            pltpu.SemaphoreType.DMA((tile_count,)),
            pltpu.SemaphoreType.DMA((tile_count,)),
            pltpu.SemaphoreType.DMA((2,)),
            pltpu.VMEM((height, 4, 128), jnp.bfloat16),
            pltpu.VMEM((height, 4, 128), jnp.bfloat16),
            pltpu.VMEM((8, 2, depth, 4, 128), jnp.bfloat16),
            pltpu.VMEM((8, 1, 128), jnp.int32),
            pltpu.SMEM((8, 1, 128), jnp.int32),
            pltpu.SemaphoreType.DMA((2, CHUNKS)),
            pltpu.SemaphoreType.DMA((2, CHUNKS)),
            pltpu.SemaphoreType.DMA((3,)),
            pltpu.SemaphoreType.DMA((8, 2)),
        ],
        compiler_params=pltpu.CompilerParams(
            collective_id=0, has_side_effects=True, vmem_limit_bytes=9 * 1024 * 1024
        ),
    )(starts, labels, sweep)
    looked = pl.pallas_call(
        functools.partial(combine_kernel, allowance),
        out_shape=jax.ShapeDtypeStruct((64, 128), jnp.float32),
        in_specs=[smem, vmem, vmem, vmem],
        out_specs=vmem,
        scratch_shapes=[
            pltpu.VMEM((2, SLOTS, SHARD_HEIGHT, 4, 128), jnp.float32),
            pltpu.SMEM((SLOTS,), jnp.int32),
            pltpu.VMEM((2, 2, 256, 128), jnp.float32),
        ],
        compiler_params=pltpu.CompilerParams(vmem_limit_bytes=12 * 1024 * 1024),
    )(arrived_labels, arrived, *pool)
    filtered = pl.pallas_call(
        filter_kernel,
        out_shape=jax.ShapeDtypeStruct((2, 64, 64), jnp.float32),
        in_specs=[vmem] * 4,
        out_specs=vmem,
        scratch_shapes=[
            pltpu.VMEM((64, 128), jnp.float32),
            pltpu.SemaphoreType.DMA,
            pltpu.SemaphoreType.DMA,
        ],
        compiler_params=pltpu.CompilerParams(collective_id=1, has_side_effects=True),
    )(looked, *transforms)
    return filtered[None, None, None]


def solution(mesh):
    if mesh.shape["pair"] != 2 or mesh.shape["ground"] != 16:
        return general(mesh)
    placed = (P("pair", "ground", None, None, None), P("ground"), P("ground", None), P("ground"))
    return jax.shard_map(
        local_pair,
        mesh=mesh,
        in_specs=placed,
        out_specs=P("pair", None, "ground", None, None, None),
        check_vma=False,
    )
```

```python
import functools
import math

import jax
import jax.numpy as jnp
import numpy as np
from jax import lax
from jax.experimental import pallas as pl
from jax.experimental.pallas import tpu as pltpu
from jax.sharding import PartitionSpec as P

LOOK_ROWS = 4
LOOK_COLS = 16
SHARD_HEIGHT = 16
TILE_ROWS = 256
TILE_COLS = 1024
SWEEP_WIDTH = 512
PATCH_SHARD_LEVEL = 16
SLOTS = 32


def multilook(reference_tiles, secondary_tiles):
    first = reference_tiles.astype(jnp.float32)
    second = secondary_tiles.astype(jnp.float32)
    real_part = first[..., 0, :] * second[..., 0, :] + first[..., 1, :] * second[..., 1, :]
    imag_part = first[..., 1, :] * second[..., 0, :] - first[..., 0, :] * second[..., 1, :]
    joined = jnp.stack([real_part, imag_part], axis=-3)
    leading = joined.shape[:-2]
    row_count = joined.shape[-2]
    col_count = joined.shape[-1]
    boxes = joined.reshape(
        leading + (row_count // LOOK_ROWS, LOOK_ROWS, col_count // LOOK_COLS, LOOK_COLS)
    )
    return jnp.mean(boxes, axis=(-3, -1))


def on_left(matrix, field):
    return jnp.einsum("ij,...jk->...ik", matrix, field, precision=lax.Precision.HIGHEST)


def on_right(field, matrix):
    return jnp.einsum("...ij,jk->...ik", field, matrix, precision=lax.Precision.HIGHEST)


def goldstein(looked):
    length = looked.shape[-1]
    positions = jnp.arange(length, dtype=jnp.int32)
    phase = positions[:, None] * positions[None, :] % length
    angle = phase.astype(jnp.float32) * (2.0 * math.pi / length)
    cosine = jnp.cos(angle)
    sine = jnp.sin(angle)
    real_in = looked[..., 0, :, :]
    imag_in = looked[..., 1, :, :]
    half_real = on_left(cosine, real_in) + on_left(sine, imag_in)
    half_imag = on_left(cosine, imag_in) - on_left(sine, real_in)
    spec_real = on_right(half_real, cosine) + on_right(half_imag, sine)
    spec_imag = on_right(half_imag, cosine) - on_right(half_real, sine)
    weight = (spec_real * spec_real + spec_imag * spec_imag + 1e-06) ** 0.25
    weight = weight / jnp.mean(weight, axis=(-2, -1), keepdims=True)
    spec_real = spec_real * weight
    spec_imag = spec_imag * weight
    back_real = on_left(cosine, spec_real) - on_left(sine, spec_imag)
    back_imag = on_left(cosine, spec_imag) + on_left(sine, spec_real)
    out_real = on_right(back_real, cosine) - on_right(back_imag, sine)
    out_imag = on_right(back_imag, cosine) + on_right(back_real, sine)
    scale = 1.0 / (length * length)
    return jnp.stack([out_real * scale, out_imag * scale], axis=-3)


def partners_of(index, pair_width):
    order = jnp.arange(pair_width, dtype=jnp.int32)
    return order + (order >= index).astype(jnp.int32)


def local(coregistered_sweeps, shard_opening_height, shard_goal_patch, shard_patch_place):
    earth_patch_total_size = lax.axis_size("ground")
    pair_count = lax.axis_size("pair")
    piece_count = shard_opening_height.shape[0]
    place_allowance = max(
        2, (2 * piece_count + earth_patch_total_size - 1) // earth_patch_total_size
    )
    sweep_resident = coregistered_sweeps[0, 0]
    target = shard_goal_patch[:, 0]
    hits = (target[:, None] == jnp.arange(earth_patch_total_size, dtype=jnp.int32)[None, :]).astype(
        jnp.int32
    )
    earlier = jnp.cumsum(hits, axis=0) - hits
    rank = jnp.sum(earlier * hits, axis=1)
    position = target * place_allowance + rank
    matches = (
        position[None, :]
        == jnp.arange(earth_patch_total_size * place_allowance, dtype=jnp.int32)[:, None]
    ).astype(jnp.int32)
    tiles_filled = jnp.sum(matches, axis=1) > 0
    chosen = jnp.sum(matches * jnp.arange(piece_count, dtype=jnp.int32)[None, :], axis=1)
    sweep_height_offset = (
        shard_opening_height[chosen][:, None] + jnp.arange(SHARD_HEIGHT, dtype=jnp.int32)[None, :]
    )
    pieces_to_send = jnp.where(
        tiles_filled[:, None, None, None],
        sweep_resident[sweep_height_offset],
        jnp.zeros((), jnp.bfloat16),
    )
    labels = jnp.where(tiles_filled, shard_patch_place[chosen] + 1, 0).astype(jnp.bfloat16)
    received_pieces, arrived_labels = (
        lax.all_to_all(
            pieces_to_send.reshape(
                earth_patch_total_size, place_allowance, SHARD_HEIGHT, 2, SWEEP_WIDTH
            ),
            "ground",
            split_axis=0,
            concat_axis=0,
            tiled=True,
        ),
        lax.all_to_all(
            labels.reshape(earth_patch_total_size, place_allowance),
            "ground",
            split_axis=0,
            concat_axis=0,
            tiled=True,
        ),
    )
    pieces_flattened = received_pieces.reshape(
        earth_patch_total_size * place_allowance, SHARD_HEIGHT * 2 * SWEEP_WIDTH
    )
    slot_labels = (jnp.arange(SLOTS, dtype=jnp.int32) + 1).astype(jnp.bfloat16)
    selector = arrived_labels.reshape(-1)[None, :] == slot_labels[:, None]
    totals = jnp.dot(
        selector.astype(jnp.bfloat16), pieces_flattened, preferred_element_type=jnp.float32
    )
    counts = jnp.sum(selector.astype(jnp.float32), axis=1)
    smoothed_pixel_mean = (totals / jnp.maximum(counts, 1.0)[:, None]).astype(jnp.bfloat16)
    ground_tile = (
        smoothed_pixel_mean.reshape(PATCH_SHARD_LEVEL, 2, SHARD_HEIGHT, 2, SWEEP_WIDTH)
        .transpose(0, 2, 3, 1, 4)
        .reshape(TILE_ROWS, 2, TILE_COLS)
    )
    pair_width = pair_count - 1
    own_refs = partners_of(lax.axis_index("pair"), pair_width)
    piece = lax.all_gather(ground_tile[None], "pair", axis=0, tiled=True)
    looked_piece = multilook(piece, ground_tile[None])
    indices = jnp.arange(piece.shape[0], dtype=jnp.int32)
    selection = (own_refs[:, None] == indices[None, :]).astype(jnp.float32)
    looked = jnp.einsum("kn,nabc->kabc", selection, looked_piece, precision=lax.Precision.HIGHEST)
    return goldstein(looked)[None, :, None]


def general(mesh):
    placed = (P("pair", "ground", None, None, None), P("ground"), P("ground", None), P("ground"))
    return jax.shard_map(
        local,
        mesh=mesh,
        in_specs=placed,
        out_specs=P("pair", None, "ground", None, None, None),
        check_vma=False,
    )


CHUNKS = 8
MESH = pl.DeviceIdType.MESH
EXACT = lax.Precision.HIGHEST


def table_kernel(allowance, opening, goal, place, starts, labels):
    tile_count = starts.shape[0]

    def clear(tile, carry):
        for slot in range(allowance):
            starts[tile, slot] = 0
            labels[tile, 0, slot] = 0
            labels[tile, 0, 2 * allowance + slot] = 0
        labels[tile, 0, allowance] = 0
        return carry

    lax.fori_loop(0, tile_count, clear, 0)

    def enter(piece, carry):
        tile = goal[piece]
        rank = labels[tile, 0, allowance]
        starts[tile, rank] = opening[piece]
        labels[tile, 0, rank] = place[piece] + 1
        labels[tile, 0, 2 * allowance + rank] = opening[piece]
        labels[tile, 0, allowance] = rank + 1
        return carry

    lax.fori_loop(0, opening.shape[0], enter, 0)


def exchange_kernel(
    allowance, starts, labels, sweep, arrived, arrived_labels,
    outgoing, send_sem, recv_sem, label_send, label_recv, own_sem,
    first_half, second_half, proxied, far_table, far_starts, burst_send, burst_recv, table_sem, proxy_sem,
):
    me = lax.axis_index("ground")
    mine = lax.axis_index("pair")
    tile_count = 16
    level = me // 4
    line = lax.rem(me, 4)
    inner = jnp.logical_or(level == 1, level == 2)
    right = level // 2
    far = 2 - right
    barrier = pltpu.get_barrier_semaphore()

    def greet(step, carry):
        pl.semaphore_signal(
            barrier, inc=1,
            device_id={"ground": lax.rem(me + step // 2, tile_count), "pair": lax.rem(mine + step, 2)},
            device_id_type=MESH,
        )
        return carry

    lax.fori_loop(1, 2 * tile_count, greet, 0)

    def extract(tile):
        def one(slot, carry):
            top = starts[tile, slot]
            for part in range(2):
                outgoing[tile, part, pl.ds(slot * SHARD_HEIGHT, SHARD_HEIGHT)] = sweep[
                    part, pl.ds(top, SHARD_HEIGHT)
                ]
            return carry

        lax.fori_loop(0, allowance, one, 0)

    def parcel(tile, other, source, source_pair):
        return pltpu.make_async_remote_copy(
            src_ref=outgoing.at[tile, other],
            dst_ref=arrived.at[source_pair, source],
            send_sem=send_sem.at[tile, other],
            recv_sem=recv_sem.at[source_pair, source],
            device_id={"ground": tile, "pair": other},
            device_id_type=MESH,
        )

    def tag(tile, source):
        return pltpu.make_async_remote_copy(
            src_ref=labels.at[tile],
            dst_ref=arrived_labels.at[source],
            send_sem=label_send.at[tile],
            recv_sem=label_recv.at[source],
            device_id={"ground": tile, "pair": mine},
            device_id_type=MESH,
        )

    far_me = far * 4 + line

    halves = (first_half, second_half)

    span = sweep.shape[1] // CHUNKS

    def burst(part, pair, chunk):
        rows = pl.ds(chunk * span, span)
        return pltpu.make_async_remote_copy(
            src_ref=sweep.at[part, rows],
            dst_ref=halves[pair].at[rows],
            send_sem=burst_send.at[part, chunk],
            recv_sem=burst_recv.at[pair, chunk],
            device_id={"ground": far_me, "pair": part},
            device_id_type=MESH,
        )

    def far_rows():
        return pltpu.make_async_remote_copy(
            src_ref=labels.at[pl.ds(8 * (1 - right), 8)],
            dst_ref=far_table,
            send_sem=table_sem.at[0],
            recv_sem=table_sem.at[1],
            device_id={"ground": far_me, "pair": mine},
            device_id_type=MESH,
        )

    def proxy(index, pair):
        return pltpu.make_async_remote_copy(
            src_ref=proxied.at[index, pair],
            dst_ref=arrived.at[pair, far_me],
            send_sem=proxy_sem.at[index, pair],
            recv_sem=recv_sem.at[pair, far_me],
            device_id={"ground": 8 * right + index, "pair": mine},
            device_id_type=MESH,
        )

    def proxy_own(pair):
        index = me - 8 * right
        return pltpu.make_async_copy(
            proxied.at[index, pair], arrived.at[pair, far_me], proxy_sem.at[index, pair]
        )

    def target_of(step):
        return lax.rem(me + step, tile_count)

    def takes(tile):
        return jnp.logical_or(jnp.logical_not(inner), tile // 8 == right)

    def send(tile):
        tag(tile, me).start()

        @pl.when(takes(tile))
        def _():
            extract(tile)
            parcel(tile, 1 - mine, me, mine).start()
            parcel(tile, mine, me, mine).start()

    pl.semaphore_wait(barrier, 2 * tile_count - 1)

    @pl.when(inner)
    def _():
        far_rows().start()
        for pair in range(2):

            @pl.when(mine == pair)
            def _():
                for part in (pair, 1 - pair):
                    for chunk in range(CHUNKS):
                        burst(part, pair, chunk).start()

        for part in range(2):
            for chunk in range(CHUNKS):
                burst(part, 0, chunk).wait_send()

    mirror = level + right * (3 - 2 * level)

    def near(step, carry):
        distance = 1 - lax.rem(step, 2)
        place = distance + mirror - 2 * distance * mirror
        tile = (place + right * (3 - 2 * place)) * 4 + lax.rem(line + 1 + step // 2, 4)

        @pl.when(tile != me)
        def _():
            send(tile)

        return carry

    def away(step, carry):
        place = 3 - lax.rem(step, 2)
        send((place + right * (3 - 2 * place)) * 4 + lax.rem(line + 1 + step // 2, 4))
        return carry

    lax.fori_loop(0, 8, near, 0)
    lax.fori_loop(0, 8, away, 0)
    extract(me)
    parcel(me, 1 - mine, me, mine).start()
    own = pltpu.make_async_copy(outgoing.at[me, mine], arrived.at[mine, me], own_sem.at[0])
    own.start()
    own_tag = pltpu.make_async_copy(labels.at[me], arrived_labels.at[me], own_sem.at[1])
    own_tag.start()

    @pl.when(inner)
    def _():
        far_rows().wait()
        rows = pltpu.make_async_copy(far_table, far_starts, table_sem.at[2])
        rows.start()
        rows.wait()

        def serve(pair):
            for chunk in range(CHUNKS):
                burst(0, pair, chunk).wait_recv()

            def one_tile(step, carry):
                index = lax.rem(4 * right + step, 8)

                def one(slot, carry):
                    top = far_starts[index, 0, 2 * allowance + slot]
                    proxied[index, pair, pl.ds(slot * SHARD_HEIGHT, SHARD_HEIGHT)] = halves[pair][
                        pl.ds(top, SHARD_HEIGHT)
                    ]
                    return carry

                lax.fori_loop(0, allowance, one, 0)

                @pl.when(8 * right + index != me)
                def _():
                    proxy(index, pair).start()

                @pl.when(8 * right + index == me)
                def _():
                    proxy_own(pair).start()

                return carry

            lax.fori_loop(0, 8, one_tile, 0)

        for first in range(2):

            @pl.when(mine == first)
            def _():
                serve(first)
                serve(1 - first)

    def finish(step, carry):
        tile = target_of(step)
        tag(tile, tile).wait_recv()
        tag(tile, me).wait_send()

        @pl.when(jnp.logical_or(jnp.logical_not(inner), tile != far_me))
        def _():
            parcel(tile, 1 - mine, tile, 1 - mine).wait_recv()
            parcel(tile, mine, tile, mine).wait_recv()

        @pl.when(takes(tile))
        def _():
            parcel(tile, 1 - mine, me, mine).wait_send()
            parcel(tile, mine, me, mine).wait_send()

        return carry

    lax.fori_loop(1, tile_count, finish, 0)
    parcel(me, 1 - mine, me, 1 - mine).wait_recv()
    parcel(me, 1 - mine, me, mine).wait_send()
    own.wait()
    own_tag.wait()

    @pl.when(inner)
    def _():
        def settle(index, carry):
            for pair in range(2):

                @pl.when(8 * right + index != me)
                def _():
                    proxy(index, pair).wait_send()

                @pl.when(8 * right + index == me)
                def _():
                    proxy_own(pair).wait()

            return carry

        lax.fori_loop(0, 8, settle, 0)


def combine_kernel(allowance, labels, arrived, spread, gather, looked, total, count, prods):
    mine = lax.axis_index("pair")
    total[...] = jnp.zeros_like(total)
    for slot in range(SLOTS):
        count[slot] = 0

    def one_source(source, carry):
        for slot in range(allowance):
            label = labels[source, 0, slot]

            @pl.when(label > 0)
            def _():
                count[label - 1] = count[label - 1] + 1
                for part in range(2):
                    piece = arrived[part, source, pl.ds(slot * SHARD_HEIGHT, SHARD_HEIGHT)]
                    total[part, label - 1] += piece.astype(jnp.float32)

        return carry

    lax.fori_loop(0, arrived.shape[1], one_source, 0)

    def one(level, carry):
        for side in range(2):
            slot = level * 2 + side
            divisor = jnp.maximum(count[slot], 1).astype(jnp.float32)
            first = (total[1, slot] / divisor).astype(jnp.bfloat16).astype(jnp.float32)
            second = (total[0, slot] / divisor).astype(jnp.bfloat16).astype(jnp.float32)
            same = first * second
            cross = first * jnp.concatenate([second[:, 2:], second[:, :2]], axis=1)
            for kind, value in ((0, same), (1, cross)):
                boxes = [jnp.sum(value[box * LOOK_ROWS : (box + 1) * LOOK_ROWS], axis=0) for box in range(4)]
                for two in range(2):
                    at = pl.ds(pl.multiple_of((level * 2 + two) * 8, 8), 8)
                    prods[side, kind, at, :] = jnp.concatenate(boxes[2 * two : 2 * two + 2], axis=0)
        return carry

    lax.fori_loop(0, PATCH_SHARD_LEVEL, one, 0)
    sub = lax.rem(lax.broadcasted_iota(jnp.int32, (256, 128), 0), 4)
    lane = lax.broadcasted_iota(jnp.int32, (256, 128), 1)
    column = lax.rem(lane, 64)
    sign = jnp.where(jnp.logical_and(lane >= 64, sub < 2), -1.0, 1.0)
    pooled = jnp.zeros((256, 128), jnp.float32)
    for side in range(2):
        wide = jnp.dot(prods[side, 0], spread[0], precision=EXACT, preferred_element_type=jnp.float32)
        wide += jnp.dot(prods[side, 1], spread[1], precision=EXACT, preferred_element_type=jnp.float32)
        pooled += jnp.where(column // 8 == side * 4 + mine * 2 + lax.rem(sub, 2), wide * sign, 0.0)
    looked[...] = jnp.dot(gather[...], pooled, precision=EXACT, preferred_element_type=jnp.float32)


def filter_kernel(looked, left, right, right_back, out, other, send_sem, recv_sem):
    mine = lax.axis_index("pair")
    barrier = pltpu.get_barrier_semaphore()
    pl.semaphore_signal(barrier, inc=1, device_id={"pair": 1 - mine}, device_id_type=MESH)
    pl.semaphore_wait(barrier, 1)
    copy = pltpu.make_async_remote_copy(
        src_ref=looked, dst_ref=other, send_sem=send_sem, recv_sem=recv_sem,
        device_id={"pair": 1 - mine}, device_id_type=MESH,
    )
    copy.start()

    def dot(a, b):
        return jnp.dot(a, b, precision=EXACT, preferred_element_type=jnp.float32)

    length = left.shape[1]
    lane = lax.broadcasted_iota(jnp.int32, (length, 2 * length), 1)
    turn = jnp.where(lane < length, 1.0, -1.0)
    flip = jnp.where(lane < length, 1.0, 1.0 - 2.0 * mine.astype(jnp.float32))
    copy.wait()
    field = (looked[...] + other[...]) * flip
    both = dot(left[...], field)
    spectrum = both[:length] + turn * pltpu.roll(both[length:], length, 1)
    spectrum = dot(spectrum, right[...])
    power = spectrum * spectrum
    power = power + pltpu.roll(power, length, 1)
    weight = jnp.sqrt(jnp.sqrt(power + 1e-06))
    mean = jnp.sum(weight) * (1.0 / (2 * length * length))
    spectrum = spectrum * (weight / mean)
    both = dot(left[...], spectrum)
    back = both[:length] - turn * pltpu.roll(both[length:], length, 1)
    back = dot(back, right_back[...]) * (1.0 / (length * length))
    out[0] = back[:, :length]
    out[1] = back[:, length:]


def constants():
    lane = np.arange(128)
    column = np.arange(64)
    pick = (lane[:, None] // LOOK_COLS == column[None, :] % 8).astype(np.float32)
    nil = np.zeros_like(pick)
    spread = np.stack([np.concatenate([pick, nil], 1), np.concatenate([nil, pick], 1)])
    gather = (column[:, None] == np.arange(256)[None, :] // 4).astype(np.float32)
    gather = gather / (LOOK_ROWS * LOOK_COLS)
    angle = (column[:, None] * column[None, :] % 64) * (2.0 * math.pi / 64)
    cosine, sine = np.cos(angle), np.sin(angle)
    left = np.concatenate([cosine, sine], 0)
    right = np.block([[cosine, -sine], [sine, cosine]])
    right_back = np.block([[cosine, sine], [-sine, cosine]])
    return (spread, gather), tuple(x.astype(np.float32) for x in (left, right, right_back))


def local_pair(coregistered_sweeps, shard_opening_height, shard_goal_patch, shard_patch_place):
    tile_count = lax.axis_size("ground")
    piece_count = shard_opening_height.shape[0]
    allowance = max(2, (2 * piece_count + tile_count - 1) // tile_count)
    pool, transforms = constants()
    smem = pl.BlockSpec(memory_space=pltpu.SMEM)
    vmem = pl.BlockSpec(memory_space=pltpu.VMEM)
    anyplace = pl.BlockSpec(memory_space=pl.ANY)
    starts, labels = pl.pallas_call(
        functools.partial(table_kernel, allowance),
        out_shape=(
            jax.ShapeDtypeStruct((tile_count, allowance), jnp.int32),
            jax.ShapeDtypeStruct((tile_count, 1, 128), jnp.int32),
        ),
        in_specs=[smem] * 3,
        out_specs=(smem, smem),
    )(shard_opening_height, shard_goal_patch[:, 0], shard_patch_place)
    height = coregistered_sweeps.shape[2]
    sweep = (
        coregistered_sweeps[0, 0]
        .reshape(height, 2, 2, 2, 128)
        .transpose(2, 0, 1, 3, 4)
        .reshape(2, height, 4, 128)
    )
    depth = allowance * SHARD_HEIGHT
    arrived, arrived_labels = pl.pallas_call(
        functools.partial(exchange_kernel, allowance),
        out_shape=(
            jax.ShapeDtypeStruct((2, tile_count, depth, 4, 128), jnp.bfloat16),
            jax.ShapeDtypeStruct((tile_count, 1, 128), jnp.int32),
        ),
        in_specs=[smem, vmem, vmem],
        out_specs=(anyplace, vmem),
        scratch_shapes=[
            pltpu.VMEM((tile_count, 2, depth, 4, 128), jnp.bfloat16),
            pltpu.SemaphoreType.DMA((tile_count, 2)),
            pltpu.SemaphoreType.DMA((2, tile_count)),
            pltpu.SemaphoreType.DMA((tile_count,)),
            pltpu.SemaphoreType.DMA((tile_count,)),
            pltpu.SemaphoreType.DMA((2,)),
            pltpu.VMEM((height, 4, 128), jnp.bfloat16),
            pltpu.VMEM((height, 4, 128), jnp.bfloat16),
            pltpu.VMEM((8, 2, depth, 4, 128), jnp.bfloat16),
            pltpu.VMEM((8, 1, 128), jnp.int32),
            pltpu.SMEM((8, 1, 128), jnp.int32),
            pltpu.SemaphoreType.DMA((2, CHUNKS)),
            pltpu.SemaphoreType.DMA((2, CHUNKS)),
            pltpu.SemaphoreType.DMA((3,)),
            pltpu.SemaphoreType.DMA((8, 2)),
        ],
        compiler_params=pltpu.CompilerParams(
            collective_id=0, has_side_effects=True, vmem_limit_bytes=9 * 1024 * 1024
        ),
    )(starts, labels, sweep)
    looked = pl.pallas_call(
        functools.partial(combine_kernel, allowance),
        out_shape=jax.ShapeDtypeStruct((64, 128), jnp.float32),
        in_specs=[smem, vmem, vmem, vmem],
        out_specs=vmem,
        scratch_shapes=[
            pltpu.VMEM((2, SLOTS, SHARD_HEIGHT, 4, 128), jnp.float32),
            pltpu.SMEM((SLOTS,), jnp.int32),
            pltpu.VMEM((2, 2, 256, 128), jnp.float32),
        ],
        compiler_params=pltpu.CompilerParams(vmem_limit_bytes=12 * 1024 * 1024),
    )(arrived_labels, arrived, *pool)
    filtered = pl.pallas_call(
        filter_kernel,
        out_shape=jax.ShapeDtypeStruct((2, 64, 64), jnp.float32),
        in_specs=[vmem] * 4,
        out_specs=vmem,
        scratch_shapes=[
            pltpu.VMEM((64, 128), jnp.float32),
            pltpu.SemaphoreType.DMA,
            pltpu.SemaphoreType.DMA,
        ],
        compiler_params=pltpu.CompilerParams(collective_id=1, has_side_effects=True),
    )(looked, *transforms)
    return filtered[None, None, None]


def solution(mesh):
    if mesh.shape["pair"] != 2 or mesh.shape["ground"] != 16:
        return general(mesh)
    placed = (P("pair", "ground", None, None, None), P("ground"), P("ground", None), P("ground"))
    return jax.shard_map(
        local_pair,
        mesh=mesh,
        in_specs=placed,
        out_specs=P("pair", None, "ground", None, None, None),
        check_vma=False,
    )
```
